128 devices in a mesh: obs: 8 (over z, core), lat: 16 (over x, y).
Axes of the slice: x: 4, y: 4, z: 4, core: 2. Of those that a mesh axis runs over, the one named last changes fastest.
Arguments:
- footprints: bfloat16 [8, 16, 384, 128, 128], P('obs', 'lat'), may hold values from -0.0546875 to 0.0546875
- block_rows: int32 [8, 16, 384], P('obs', 'lat'), may hold values from 0 to 31
- block_cols: int32 [8, 16, 384], P('obs', 'lat'), may hold values from 0 to 639
- block_scale: int32 [8, 16, 384], P('obs', 'lat'), may hold values from 0 to 3
- lat_width: int32 [512], replicated, may hold values from 1 to 32, as said below
- lon_width: int32 [512], replicated, may hold values from 1 to 80
- obs_weight: float32 [32768], P('obs'), may hold values from 0.3 to 3
- solution: float32 [8, 4, 512, 640], P(None, None, 'lat'), may hold values from -6 to 6
- residual: float32 [8, 4, 512, 640], P(None, None, 'lat'), may hold values from -6 to 6
- direction: float32 [8, 4, 512, 640], P(None, None, 'lat'), may hold values from -6 to 6
Outputs:
- next_solution: float32 [8, 4, 512, 640], P(None, None, 'lat')
- next_residual: float32 [8, 4, 512, 640], P(None, None, 'lat')
- next_direction: float32 [8, 4, 512, 640], P(None, None, 'lat')
The draws below stay inside these ranges and needn't reach their ends.
Inputs may be any that keep to these rules, and one draw needn't show every extreme that they name: `lat_width`: some latitude row has band width exactly 32.
All inputs are finite; a program needn't handle non-finite values.
Results may differ from the reference program's by a relative error of at most 0.00039.
Values may be sent and summed in bfloat16 or wider, within the bound.
A program may use at most 128 MiB of HBM per device.

```python
import math
import jax
import jax.numpy as jnp
from jax import lax

K = 8
BLOCK = 128
RB_DEV = 32
LAT_DEV = 32
NLON = 640
WEEKS = 4
NBLK = 384
OBS_DEV = 4096
SOUNDINGS = 32768
NLAT = 512
CB_DEV = 640
N_OBS = 8
N_LAT = 16


def draw_lat_width(key, part):
    first_key = jax.random.fold_in(key, 11)
    second_key = jax.random.fold_in(key, 23)
    widths = jax.random.randint(first_key, (NLAT,), 1, LAT_DEV + 1)
    chosen = jax.random.randint(second_key, (), 0, NLAT)
    widths = widths.at[chosen].set(LAT_DEV)
    return widths.astype(jnp.int32)


def with_ends(result, own_key, least, top_value):
    dims = result.shape
    spot = [jax.random.randint(jax.random.fold_in(own_key, axis), (), 0, dims[axis]) for axis in range(len(dims))]
    result = result.at[tuple(spot)].set(least)
    longest = dims.index(max(dims))
    spot[longest] = (spot[longest] + 1) % dims[longest]
    return result.at[tuple(spot)].set(top_value)


def block_levels(key, extent, pieces, low, high):
    loudness, own = 1.0, jax.random.fold_in(key, 6)
    for dim, shards_of in pieces:
        steps = jnp.exp(jax.random.uniform(jax.random.fold_in(own, dim), (shards_of,), jnp.float32, low / len(pieces), high / len(pieces)))
        loudness = loudness * jnp.repeat(steps, extent[dim] // shards_of).reshape([-1 if axis == dim else 1 for axis in range(len(extent))])
    return loudness


def gaussian(rng, extent, scale, limit, cuts=(), held_as=jnp.bfloat16):
    drawn = scale * jax.random.normal(rng, extent, jnp.float32)
    if cuts:
        drawn = drawn * block_levels(rng, extent, cuts, -0.22, 0.18)
    return jnp.clip(drawn, -limit, limit).astype(held_as)


def setup_inputs(seed: int = 0) -> dict:
    key_list = jax.random.split(jax.random.key(seed), 11)
    return {
        "footprints": gaussian(key_list[0], (N_OBS, N_LAT, NBLK, BLOCK, BLOCK), (BLOCK * NBLK * N_LAT // (2 * RB_DEV)) ** -0.5, 0.0546875, ((0, 8), (1, 16))),
        "block_rows": with_ends(jax.random.randint(key_list[1], (N_OBS, N_LAT, NBLK), 0, RB_DEV), jax.random.fold_in(key_list[1], 1), 0, RB_DEV - 1).astype(jnp.int32),
        "block_cols": with_ends(jax.random.randint(key_list[2], (N_OBS, N_LAT, NBLK), 0, CB_DEV), jax.random.fold_in(key_list[2], 1), 0, CB_DEV - 1).astype(jnp.int32),
        "block_scale": with_ends(jax.random.randint(key_list[3], (N_OBS, N_LAT, NBLK), 0, 4), jax.random.fold_in(key_list[3], 1), 0, 3).astype(jnp.int32),
        "lat_width": draw_lat_width(jax.random.fold_in(key_list[10], 71), 0),
        "lon_width": with_ends(jax.random.randint(key_list[5], (NLAT,), 1, NLON // 8 + 1), jax.random.fold_in(key_list[5], 1), 1, (NLON // 8 + 1) - 1).astype(jnp.int32),
        "obs_weight": jnp.clip(jnp.exp(math.log(3.0) - 2.3025851 * jax.random.uniform(key_list[6], (SOUNDINGS,), jnp.float32) ** block_levels(key_list[6], (SOUNDINGS,), ((0, 8),), -0.2, 0.2)), 0.3, 3.0),
        "solution": gaussian(key_list[7], (K, WEEKS, NLAT, NLON), 1.0, 6.0, ((2, 16),), jnp.float32),
        "residual": gaussian(key_list[8], (K, WEEKS, NLAT, NLON), 1.0, 6.0, ((2, 16),), jnp.float32),
        "direction": gaussian(key_list[9], (K, WEEKS, NLAT, NLON), 1.0, 6.0, ((2, 16),), jnp.float32),
    }


def lat_matrix(index_out, width_out, index_in, row_reach):
    decay_rows = row_reach / 2.0
    distance = jnp.abs(index_out[:, None] - index_in[None, :]).astype(jnp.float32)
    offsets = jnp.abs(jnp.arange(-row_reach, row_reach + 1)).astype(jnp.float32)
    limits = width_out.astype(jnp.float32)[:, None]
    weights = jnp.where(offsets[None, :] <= limits, jnp.exp(-2.0 * offsets / decay_rows)[None, :], 0.0)
    normal = jnp.sqrt(lax.optimization_barrier(jnp.sum(weights, axis=1)))
    return jnp.where(distance <= limits, jnp.exp(-distance / decay_rows), 0.0) / normal[:, None]

def lon_matrix(row_width, lon_points):
    lon_decay = lon_points / 32.0
    lon_reach = lon_points // 8
    lon_grid = jnp.arange(lon_points)
    apart_cells = jnp.abs(lon_grid[:, None] - lon_grid[None, :])
    apart_cells = jnp.minimum(apart_cells, lon_points - apart_cells).astype(jnp.float32)
    offsets = jnp.abs(jnp.arange(-lon_reach, lon_reach + 1)).astype(jnp.float32)
    limit_cells = row_width.astype(jnp.float32)
    normal = jnp.sqrt(jnp.sum(jnp.where(offsets <= limit_cells, jnp.exp(-2.0 * offsets / lon_decay), 0.0)))
    return jnp.where(apart_cells <= limit_cells, jnp.exp(-apart_cells / lon_decay), 0.0) / normal

def lon_apply(field_in, widths):
    lon_points = field_in.shape[3]

    def one_row(packed):
        slab_row, row_width = packed
        return jnp.einsum('kwa,ab->kwb', slab_row, lon_matrix(row_width, lon_points), precision=lax.Precision.HIGHEST)
    mixed_rows = lax.map(one_row, (jnp.moveaxis(field_in, 2, 0), widths))
    return jnp.moveaxis(mixed_rows, 0, 2)

def inner_gram(left_field, right_field):
    left_rows = left_field.reshape(left_field.shape[0], -1)
    right_rows = right_field.reshape(right_field.shape[0], -1)
    return jnp.einsum('kx,jx->kj', left_rows, right_rows, precision=lax.Precision.HIGHEST)

def combine_columns(coeffs, field_in):
    return jnp.einsum('ba,bwix->awix', coeffs, field_in, precision=lax.Precision.HIGHEST)

def reference(footprints, block_rows, block_cols, block_scale, lat_width, lon_width, obs_weight, solution, residual, direction):
    highest = lax.Precision.HIGHEST
    lat_index = jnp.arange(NLAT)
    lat_full = lat_matrix(lat_index, lat_width, lat_index, LAT_DEV)
    spread = jnp.einsum('ij,kwjl->kwil', lat_full, lon_apply(direction, lon_width), precision=highest)
    band_cells = spread.astype(jnp.bfloat16).reshape(K, WEEKS, N_LAT, LAT_DEV, NLON)
    band_cells = jnp.moveaxis(band_cells, 2, 0).reshape(N_LAT, K, CB_DEV, BLOCK)
    flat_blocks = footprints.reshape(N_OBS * N_LAT, NBLK, BLOCK, BLOCK)
    flat_rows = block_rows.reshape(N_OBS * N_LAT, NBLK)
    flat_cols = block_cols.reshape(N_OBS * N_LAT, NBLK)
    flat_scale = jnp.exp2(-block_scale.reshape(N_OBS * N_LAT, NBLK).astype(jnp.float32))
    row_slots = jnp.arange(RB_DEV)
    col_slots = jnp.arange(CB_DEV)

    def forward_one(device_slot):
        blocks = flat_blocks[device_slot].astype(jnp.float32)
        picked = jnp.take(band_cells[device_slot % N_LAT], flat_cols[device_slot], axis=1).astype(jnp.float32)
        partial_value = jnp.einsum('nrc,knc->knr', blocks, picked) * flat_scale[device_slot][None, :, None]
        row_hot = (flat_rows[device_slot][:, None] == row_slots[None, :]).astype(jnp.float32)
        return jnp.einsum('knr,nb->kbr', partial_value, row_hot, precision=highest).reshape(K, OBS_DEV)
    partials = lax.map(forward_one, jnp.arange(N_OBS * N_LAT))
    obs_sums = lax.optimization_barrier(jnp.sum(partials.reshape(N_OBS, N_LAT, K, OBS_DEV), axis=1))
    obs_values = (obs_sums * obs_weight.reshape(N_OBS, 1, OBS_DEV)).astype(jnp.bfloat16)

    def adjoint_one(device_slot):
        blocks = flat_blocks[device_slot].astype(jnp.float32)
        slab_values = obs_values[device_slot // N_LAT].reshape(K, RB_DEV, BLOCK)
        pulled = jnp.take(slab_values, flat_rows[device_slot], axis=1).astype(jnp.float32)
        adjoint_terms = jnp.einsum('nrc,knr->knc', blocks, pulled) * flat_scale[device_slot][None, :, None]
        col_hot = (flat_cols[device_slot][:, None] == col_slots[None, :]).astype(jnp.float32)
        return jnp.einsum('knc,nb->kbc', adjoint_terms, col_hot, precision=highest)
    adjoints = lax.map(adjoint_one, jnp.arange(N_OBS * N_LAT)).reshape(N_OBS, N_LAT, K, CB_DEV, BLOCK)
    adjoint = lax.optimization_barrier(jnp.sum(adjoints, axis=0)).reshape(N_LAT, K, WEEKS, LAT_DEV, NLON)
    adjoint = jnp.moveaxis(adjoint, 0, 2).reshape(K, WEEKS, NLAT, NLON)
    pulled_back = jnp.einsum('ji,kwjl->kwil', lat_full, adjoint, precision=highest)
    image = direction + lon_apply(pulled_back, lon_width)
    gram_old = inner_gram(residual, residual)
    curvature = inner_gram(direction, image)
    step_coef = jax.scipy.linalg.cho_solve((jnp.linalg.cholesky(curvature), True), gram_old)
    next_solution = solution + combine_columns(step_coef, direction)
    next_residual = residual - combine_columns(step_coef, image)
    gram_new = inner_gram(next_residual, next_residual)
    turn_coef = jax.scipy.linalg.cho_solve((jnp.linalg.cholesky(gram_old), True), gram_new)
    next_direction = next_residual + combine_columns(turn_coef, direction)
    return (next_solution, next_residual, next_direction)
```

```python
import functools

import jax
import jax.numpy as jnp
from jax import lax
from jax.experimental import pallas as pl
from jax.experimental.pallas import tpu as pltpu
from jax.sharding import PartitionSpec as P

MESH = pl.DeviceIdType.MESH
HIGHEST = lax.Precision.HIGHEST
F32 = jnp.float32
BF16 = jnp.bfloat16
VMEM = pltpu.VMEM
DMA = pltpu.SemaphoreType.DMA
EDGE = 128
CHIPS = 4
ANY_SPEC = pl.BlockSpec(memory_space=pl.ANY)
VMEM_SPEC = pl.BlockSpec(memory_space=pltpu.VMEM)
SMEM_SPEC = pl.BlockSpec(memory_space=pltpu.SMEM)
HALF = 320


def iota(shape, axis):
    return lax.broadcasted_iota(jnp.int32, shape, axis)


def norm_of(width, decay):
    p = jnp.exp(jnp.full_like(width, -2.0 / decay))
    return jnp.sqrt(1.0 + 2.0 * p * (1.0 - jnp.exp(width * (-2.0 / decay))) / (1.0 - p))


def down_rows(row):
    return jnp.transpose(jnp.broadcast_to(row, (EDGE, EDGE)))


def along_lon(blocks, width, decay, bits):
    rows = blocks[0].shape[0]
    count = len(blocks)
    lane = iota((rows, EDGE), 1)
    terms = width.astype(jnp.int32) + 1
    picks = [((terms >> m) & 1) == 1 for m in range(bits)]

    def shifted(values, step, sign):
        turned = [pltpu.roll(v, step if sign > 0 else EDGE - step, 1) for v in values]
        inside = lane >= step if sign > 0 else lane < EDGE - step
        return [jnp.where(inside, turned[b], turned[(b - sign) % count]) for b in range(count)]

    sides = []
    for sign in (1, -1):
        power = blocks
        total = [jnp.where(picks[0], v, 0.0) for v in blocks]
        for m in range(1, bits):
            half = 2 ** (m - 1)
            moved = shifted(power, half, sign)
            fade = jnp.exp(jnp.full((rows, EDGE), -half / decay, F32))
            power = [a + fade * c for a, c in zip(power, moved)]
            moved = shifted(total, 2 * half, sign)
            fade = fade * fade
            total = [jnp.where(picks[m], a + fade * c, t) for a, c, t in zip(power, moved, total)]
        sides.append(total)
    scale = 1.0 / norm_of(width, decay)
    return [(up + down - x) * scale for up, down, x in zip(sides[0], sides[1], blocks)]


def lat_block(offset, width, decay, present, transposed):
    r, c = iota((EDGE, EDGE), 0), iota((EDGE, EDGE), 1)
    same = (r // 32) == (c // 32)
    distance = jnp.abs((r % 32) - (c % 32) - 32 * offset).astype(F32)
    value = jnp.exp(-distance / decay) / norm_of(width, decay)
    keep = jnp.where(same & (distance <= width), value, 0.0)
    if present is not None:
        keep = jnp.where(present, keep, 0.0)
    return keep


def greet(peers):
    barrier = pltpu.get_barrier_semaphore()
    for peer in peers:
        pl.semaphore_signal(barrier, inc=1, device_id=peer, device_id_type=MESH)
    pl.semaphore_wait(barrier, len(peers))


def obs_peers(o):
    z, c = o // 2, o % 2

    def at(step, core):
        return ((z + step + CHIPS) % CHIPS) * 2 + core

    return z, c, at


def gather_over_obs(own_ref, out_ref, o, send, recv, local):
    z, c, at = obs_peers(o)
    other = 1 - c
    partner, up, down = at(0, other), at(1, c), at(-1, c)
    first, second = pl.ds(0, HALF), pl.ds(HALF, HALF)

    def copy(role, src, dst, to):
        return pltpu.make_async_remote_copy(
            src_ref=src, dst_ref=dst, send_sem=send.at[role], recv_sem=recv.at[role],
            device_id={"obs": to}, device_id_type=MESH,
        )

    def spot(step, core, rows=None):
        return out_ref.at[at(step, core)] if rows is None else out_ref.at[at(step, core), rows]

    def moved(role, step, core, rows, to):
        ref = spot(step, core, rows)
        return copy(role, ref, ref, to)

    keep = pltpu.make_async_copy(own_ref, out_ref.at[o], local)
    started = [copy(1, own_ref, out_ref.at[o], up), copy(2, own_ref, out_ref.at[o], down), copy(0, own_ref, out_ref.at[o], partner)]
    for one in started:
        one.start()
    keep.start()
    copy(1, own_ref, spot(-1, c), up).wait_recv()
    batch = [moved(3, -1, c, first, up), moved(5, -1, c, None, partner)]
    for one in batch:
        one.start()
    started += batch
    copy(2, own_ref, spot(1, c), down).wait_recv()
    batch = [moved(4, 1, c, second, down), moved(6, 1, c, None, partner)]
    for one in batch:
        one.start()
    started += batch
    copy(3, spot(2, c, first), spot(2, c, first), up).wait_recv()
    one = moved(7, 2, c, first, partner)
    one.start()
    started.append(one)
    copy(4, spot(2, c, second), spot(2, c, second), down).wait_recv()
    one = moved(8, 2, c, second, partner)
    one.start()
    started.append(one)
    copy(0, own_ref, spot(0, other), partner).wait_recv()
    moved(5, -1, other, None, partner).wait_recv()
    moved(6, 1, other, None, partner).wait_recv()
    moved(7, 2, other, first, partner).wait_recv()
    moved(8, 2, other, second, partner).wait_recv()
    for one in started:
        one.wait_send()
    keep.wait()


def halo_copies(src_ref, halo_ref, l, count, send, recv):
    result = []
    for slot, step in ((0, 1), (1, count - 1)):
        result.append(pltpu.make_async_remote_copy(
            src_ref=src_ref, dst_ref=halo_ref.at[slot], send_sem=send.at[slot], recv_sem=recv.at[slot],
            device_id={"lat": (l + step) % count}, device_id_type=MESH,
        ))
    return result


def spread_kernel(sizes, direction_ref, widths_ref, out_ref, field, smooth, wire, halo, shard, send, recv, hsend, hrecv, local):
    o, l = lax.axis_index("obs"), lax.axis_index("lat")
    bands, weeks, lon_blocks, bits, lat_decay, lon_decay = sizes
    load = pltpu.make_async_copy(direction_ref.at[o], field, local)
    load.start()
    z, c, at = obs_peers(o)
    greet([{"obs": at(0, 1 - c)}, {"obs": at(1, c)}, {"obs": at(-1, c)},
           {"lat": (l + 1) % bands}, {"lat": (l + bands - 1) % bands}])
    lon_rows = down_rows(widths_ref[0:1, :])[0:32]
    load.wait()

    @pl.loop(0, weeks)
    def _(w):
        blocks = [field[w, :, b * EDGE:(b + 1) * EDGE] for b in range(lon_blocks)]
        done = along_lon(blocks, lon_rows, lon_decay, bits)
        for b in range(lon_blocks):
            rows = pl.ds(pl.multiple_of(b * EDGE + w * 32, 32), 32)
            smooth[rows, :] = done[b]
            wire[rows, :] = done[b].astype(wire.dtype)

    copies = halo_copies(wire, halo, l, bands, hsend, hrecv)
    for one in copies:
        one.start()
    own_rows = down_rows(widths_ref[2:3, :])
    mid = lat_block(0, own_rows, lat_decay, None, False)
    low = lat_block(-1, own_rows, lat_decay, l > 0, False)
    high = lat_block(1, own_rows, lat_decay, l < bands - 1, False)
    dot = functools.partial(jnp.dot, precision=HIGHEST, preferred_element_type=F32)
    near = [dot(mid, smooth[b * EDGE:(b + 1) * EDGE, :]) for b in range(lon_blocks)]
    for one in copies:
        one.wait_recv()
    for b in range(lon_blocks):
        rows = slice(b * EDGE, (b + 1) * EDGE)
        total = near[b] + dot(low, halo[0, rows, :].astype(F32)) + dot(high, halo[1, rows, :].astype(F32))
        shard[rows, :] = total.astype(shard.dtype)
    gather_over_obs(shard, out_ref, o, send, recv, local)
    for one in copies:
        one.wait_send()


def forward_kernel(per_step, rows_ref, cols_ref, scale_ref, cells_ref, blocks_ref, out_ref, cells):
    step = pl.program_id(0)

    @pl.when(step == 0)
    def _():
        cells[...] = cells_ref[...].astype(F32)
        out_ref[...] = jnp.zeros_like(out_ref)

    def one(n, carry):
        at = step * per_step + n
        col = cols_ref[at]
        start = (col % 5) * EDGE + col // 5
        picked = cells[pl.ds(start, 8, stride=640), :].astype(BF16)
        value = lax.dot_general(picked, blocks_ref[n], (((1,), (1,)), ((), ())), preferred_element_type=F32)
        factor = (8 >> scale_ref[at]).astype(F32) * 0.125
        row = rows_ref[at]
        out_ref[row] = out_ref[row] + value * factor
        return carry

    lax.fori_loop(0, per_step, one, 0, unroll=8)


def adjoint_kernel(per_step, rows_ref, cols_ref, scale_ref, values_ref, blocks_ref, out_ref):
    step = pl.program_id(0)

    @pl.when(step == 0)
    def _():
        out_ref[...] = jnp.zeros_like(out_ref)

    def one(n, carry):
        at = step * per_step + n
        col = cols_ref[at]
        start = (col % 5) * EDGE + col // 5
        value = jnp.dot(values_ref[rows_ref[at]], blocks_ref[n], preferred_element_type=F32)
        factor = (8 >> scale_ref[at]).astype(F32) * 0.125
        place = pl.ds(start, 8, stride=640)
        out_ref[place, :] = out_ref[place, :] + value * factor
        return carry

    lax.fori_loop(0, per_step, one, 0, unroll=8)


def sum_bands_kernel(bands, part_ref, weight_ref, out_ref, got, shard, send, recv, send2, recv2):
    l = lax.axis_index("lat")
    share = part_ref.shape[0] // bands
    greet([{"lat": (l + d) % bands} for d in range(1, bands)])
    mine = pl.ds(l * share, share)

    def first(d):
        peer = (l + d) % bands
        return pltpu.make_async_remote_copy(
            src_ref=part_ref.at[pl.ds(peer * share, share)], dst_ref=got.at[d], send_sem=send.at[d], recv_sem=recv.at[d],
            device_id={"lat": peer}, device_id_type=MESH,
        )

    def second(d, owner):
        return pltpu.make_async_remote_copy(
            src_ref=shard, dst_ref=out_ref.at[pl.ds(owner * share, share)], send_sem=send2.at[d], recv_sem=recv2.at[d],
            device_id={"lat": (l + d) % bands}, device_id_type=MESH,
        )

    for d in range(1, bands):
        first(d).start()
    total = part_ref[mine]
    for d in range(1, bands):
        first(d).wait_recv()
        total = total + got[d]
    weight = weight_ref[mine]
    shard[...] = (total * weight).astype(shard.dtype)
    for d in range(1, bands):
        second(d, l).start()
    out_ref[mine] = shard[...]
    for d in range(1, bands):
        second(d, (l + bands - d) % bands).wait_recv()
    for d in range(1, bands):
        first(d).wait_send()
        second(d, l).wait_send()


def image_kernel(sizes, part_ref, widths_ref, out_ref, own, there, chip, got_half, got_full, band, halo, shard,
                 send, recv, hsend, hrecv, psend, precv, rsend, rrecv, load, local):
    o, l = lax.axis_index("obs"), lax.axis_index("lat")
    bands, weeks, lon_blocks, bits, lat_decay, lon_decay = sizes
    z, c, at = obs_peers(o)
    other = 1 - c
    partner, up, down = at(0, other), at(1, c), at(-1, c)
    greet([{"obs": partner}, {"obs": up}, {"obs": down},
           {"lat": (l + 1) % bands}, {"lat": (l + bands - 1) % bands}])
    order = (2, 1, 3, 0)

    def swap(s):
        return pltpu.make_async_remote_copy(
            src_ref=part_ref.at[at(s, other)], dst_ref=there.at[s], send_sem=psend.at[s], recv_sem=precv.at[s],
            device_id={"obs": partner}, device_id_type=MESH,
        )

    def fetch(s):
        return pltpu.make_async_copy(part_ref.at[at(s, c)], own.at[s], load.at[s])

    for s in order:
        swap(s).start()
        fetch(s).start()

    def ring(role, src, dst, to):
        return pltpu.make_async_remote_copy(
            src_ref=src, dst_ref=dst, send_sem=rsend.at[role], recv_sem=rrecv.at[role],
            device_id={"obs": to}, device_id_type=MESH,
        )

    def arrive(s):
        swap(s).wait_recv()
        fetch(s).wait()

    first, second = pl.ds(0, HALF), pl.ds(HALF, HALF)
    far_up = ring(0, chip.at[2, first], got_half.at[0], up)
    far_down = ring(1, chip.at[2, second], got_half.at[1], down)
    near_up = ring(2, chip.at[1], got_full.at[0], up)
    near_down = ring(3, chip.at[3], got_full.at[1], down)
    arrive(2)
    chip[2] = (own[2] + there[2]).astype(chip.dtype)
    far_up.start()
    far_down.start()
    arrive(1)
    chip[1, HALF:, :] = (own[1, HALF:, :] + there[1, HALF:, :]).astype(chip.dtype)
    arrive(3)
    chip[3, :HALF, :] = (own[3, :HALF, :] + there[3, :HALF, :]).astype(chip.dtype)
    far_up.wait_recv()
    chip[1, :HALF, :] = (own[1, :HALF, :] + there[1, :HALF, :] + got_half[0].astype(F32)).astype(chip.dtype)
    near_up.start()
    far_down.wait_recv()
    chip[3, HALF:, :] = (own[3, HALF:, :] + there[3, HALF:, :] + got_half[1].astype(F32)).astype(chip.dtype)
    near_down.start()
    arrive(0)
    own[0] = own[0] + there[0]
    dot = functools.partial(jnp.dot, precision=HIGHEST, preferred_element_type=F32)
    low = lat_block(-1, widths_ref[1:2, :], lat_decay, l > 0, True)
    mid = lat_block(0, widths_ref[2:3, :], lat_decay, None, True)
    high = lat_block(1, widths_ref[3:4, :], lat_decay, l < bands - 1, True)
    near_up.wait_recv()
    near_down.wait_recv()
    total = own[0] + got_full[0].astype(F32) + got_full[1].astype(F32)
    own[0] = total
    band[...] = total.astype(band.dtype)
    copies = halo_copies(band, halo, l, bands, hsend, hrecv)
    for one in copies:
        one.start()
    near = [dot(mid, own[0, b * EDGE:(b + 1) * EDGE, :]) for b in range(lon_blocks)]
    for one in copies:
        one.wait_recv()
    for b in range(lon_blocks):
        rows = slice(b * EDGE, (b + 1) * EDGE)
        own[1, rows, :] = near[b] + dot(low, halo[0, rows, :].astype(F32)) + dot(high, halo[1, rows, :].astype(F32))
    lon_rows = down_rows(widths_ref[0:1, :])[0:32]

    @pl.loop(0, weeks)
    def _(w):
        places = [pl.ds(pl.multiple_of(b * EDGE + w * 32, 32), 32) for b in range(lon_blocks)]
        done = along_lon([own[1, place, :] for place in places], lon_rows, lon_decay, bits)
        for place, value in zip(places, done):
            shard[place, :] = value.astype(shard.dtype)

    gather_over_obs(shard, out_ref, o, send, recv, local)
    for one in copies + [far_up, far_down, near_up, near_down]:
        one.wait_send()
    for s in order:
        swap(s).wait_send()


def gram_kernel(k, residual_ref, direction_ref, change_ref, out_ref, sums):
    step = pl.program_id(0)
    lon_blocks = change_ref.shape[1]

    @pl.when(step == 0)
    def _():
        sums[...] = jnp.zeros_like(sums)

    def one(b, carry):
        lanes = pl.ds(pl.multiple_of(b * EDGE, EDGE), EDGE)
        res = [residual_ref[i, 0, :, lanes] for i in range(k)]
        dire = [direction_ref[i, 0, :, lanes] for i in range(k)]
        img = [dire[i] + change_ref[i, b].astype(F32) for i in range(k)]

        def add(t, i, j, x, y):
            sums[t, i, j] = sums[t, i, j] + jnp.sum((x * y).reshape(4, 8, EDGE), axis=0)

        for i in range(k):
            for j in range(k):
                if i <= j:
                    add(0, i, j, res[i], res[j])
                    add(3, i, j, img[i], img[j])
                add(1, i, j, dire[i], img[j])
                add(2, i, j, img[i], res[j])
        return carry

    lax.fori_loop(0, lon_blocks, one, 0)

    @pl.when(step == pl.num_programs(0) - 1)
    def _():
        lane, row = iota((k, EDGE), 1), iota((k, EDGE), 0)
        result = jnp.zeros((k, EDGE), F32)
        for t in range(4):
            for i in range(k):
                line = jnp.sum(jnp.sum(sums[t, i], axis=1), axis=1, keepdims=True)
                line = jnp.broadcast_to(line, (k, EDGE))
                result = jnp.where(lane == t * k + i, line, result)
        out_ref[...] = result


def flip(x):
    square = jnp.concatenate([x, jnp.zeros((EDGE - 8, EDGE), F32)], axis=0)
    return jnp.transpose(square)[:8, :]


def product(x, y):
    return sum(jnp.broadcast_to(x[:, i:i + 1], (8, EDGE)) * jnp.broadcast_to(y[i:i + 1, :], (8, EDGE)) for i in range(8))


def solve(a, b):
    row = iota((8, EDGE), 0)
    for p in range(8):
        line = jnp.broadcast_to(a[p:p + 1, :], (8, EDGE))
        line_b = jnp.broadcast_to(b[p:p + 1, :], (8, EDGE))
        column = jnp.broadcast_to(a[:, p:p + 1], (8, EDGE))
        inverse = 1.0 / jnp.broadcast_to(a[p:p + 1, p:p + 1], (8, EDGE))
        ratio = column * inverse
        here = row == p
        a = jnp.where(here, line * inverse, a - ratio * line)
        b = jnp.where(here, line_b * inverse, b - ratio * line_b)
    return b


def solve_kernel(bands, part_ref, out_ref, got, send, recv):
    l = lax.axis_index("lat")
    greet([{"lat": (l + d) % bands} for d in range(1, bands)])

    def to(d):
        return pltpu.make_async_remote_copy(
            src_ref=part_ref, dst_ref=got.at[l], send_sem=send.at[d], recv_sem=recv.at[d],
            device_id={"lat": (l + d) % bands}, device_id_type=MESH,
        )

    for d in range(1, bands):
        to(d).start()
    got[l] = part_ref[...]
    for d in range(1, bands):
        to(d).wait_recv()
    total = got[0]
    for d in range(1, bands):
        total = total + got[d]
    lane, row = iota((8, EDGE), 1), iota((8, EDGE), 0)
    parts = []
    for t in range(4):
        moved = total if t == 0 else pltpu.roll(total, EDGE - 8 * t, 1)
        parts.append(jnp.where(lane < 8, moved, 0.0))

    def full(x):
        low = jnp.where(lane <= row, x, 0.0)
        return low + flip(jnp.where(lane < row, x, 0.0))

    gram_old, image_image = full(parts[0]), full(parts[3])
    curvature = 0.5 * (parts[1] + flip(parts[1]))
    residual_image = parts[2]
    step = solve(curvature, gram_old)
    cross = product(residual_image, step)
    gram_new = gram_old - cross - flip(cross) + product(flip(step), product(image_image, step))
    turn = solve(gram_old, gram_new)
    out_ref[...] = jnp.where(lane < 8, step, 0.0) + pltpu.roll(jnp.where(lane < 8, turn, 0.0), 8, 1)
    for d in range(1, bands):
        to(d).wait_send()


def update_kernel(k, coef_ref, solution_ref, residual_ref, direction_ref, change_ref, sol_out, res_out, dir_out):
    lon_blocks = change_ref.shape[1]

    def one(b, carry):
        lanes = pl.ds(pl.multiple_of(b * EDGE, EDGE), EDGE)
        for r in range(4):
            rows = slice(r * 8, r * 8 + 8)
            dire = [direction_ref[i, 0, rows, lanes] for i in range(k)]
            img = [dire[i] + change_ref[i, b, rows, :].astype(F32) for i in range(k)]
            for a in range(k):
                forth = sum(coef_ref[i, a] * dire[i] for i in range(k))
                back = sum(coef_ref[i, a] * img[i] for i in range(k))
                turn = sum(coef_ref[i, k + a] * dire[i] for i in range(k))
                left = residual_ref[a, 0, rows, lanes] - back
                sol_out[a, 0, rows, lanes] = solution_ref[a, 0, rows, lanes] + forth
                res_out[a, 0, rows, lanes] = left
                dir_out[a, 0, rows, lanes] = left + turn
        return carry

    lax.fori_loop(0, lon_blocks, one, 0)


WIRE_OUT = F32
WIRE_SUM = F32
WIRE_BACK = F32
WIRE_IMAGE = F32


def params(collective=None, limit=None):
    extra = {} if collective is None else {"collective_id": collective, "has_side_effects": True}
    return pltpu.CompilerParams(vmem_limit_bytes=limit or (48 << 20), **extra)


def shards(bands, footprints, block_rows, block_cols, block_scale, lat_width, lon_width, obs_weight, solution, residual, direction):
    k, weeks, band_rows, nlon = direction.shape
    blocks = footprints.shape[2]
    lon_blocks = nlon // EDGE
    field_rows = weeks * band_rows * lon_blocks
    assert (k, weeks, band_rows, field_rows) == (8, 4, 32, 2 * HALF)
    row_blocks = obs_weight.shape[0] // EDGE
    sizes = (bands, weeks, lon_blocks, (nlon // 8 + 1).bit_length(), band_rows / 2.0, nlon / 32.0)
    l = lax.axis_index("lat")
    around = jnp.pad(lat_width.reshape(bands, band_rows), ((1, 1), (0, 0)))
    near = jnp.concatenate([
        lax.dynamic_slice_in_dim(lon_width.reshape(bands, band_rows), l, 1),
        lax.dynamic_slice_in_dim(around, l, 3),
    ])
    widths = jnp.pad(jnp.tile(near, (1, weeks)), ((0, 4), (0, 0))).astype(F32)
    rows, cols, scale = block_rows.reshape(blocks), block_cols.reshape(blocks), block_scale.reshape(blocks)
    field = (field_rows, EDGE)

    cells = pl.pallas_call(
        functools.partial(spread_kernel, sizes),
        out_shape=jax.ShapeDtypeStruct((k, *field), BF16),
        in_specs=[ANY_SPEC, VMEM_SPEC],
        out_specs=ANY_SPEC,
        scratch_shapes=[
            VMEM((weeks, band_rows, nlon), F32), VMEM(field, F32), VMEM(field, WIRE_OUT), VMEM((2, *field), WIRE_OUT),
            VMEM(field, BF16), DMA((9,)), DMA((9,)), DMA((2,)), DMA((2,)), DMA(()),
        ],
        compiler_params=params(1),
        name="spread",
    )(direction, widths)

    per_step = 48
    smem = [SMEM_SPEC] * 3
    block_spec = pl.BlockSpec((None, None, per_step, EDGE, EDGE), lambda i: (0, 0, i, 0, 0))
    forward = pl.pallas_call(
        functools.partial(forward_kernel, per_step),
        grid=(blocks // per_step,),
        out_shape=jax.ShapeDtypeStruct((row_blocks, k, EDGE), F32),
        in_specs=smem + [pl.BlockSpec((k * field_rows, EDGE), lambda i: (0, 0)), block_spec],
        out_specs=pl.BlockSpec((row_blocks, k, EDGE), lambda i: (0, 0, 0)),
        scratch_shapes=[VMEM((k * field_rows, EDGE), F32)],
        compiler_params=params(),
        name="forward",
    )(rows, cols, scale, cells.reshape(k * field_rows, EDGE), footprints)

    share = row_blocks // bands
    values = pl.pallas_call(
        functools.partial(sum_bands_kernel, bands),
        out_shape=jax.ShapeDtypeStruct((row_blocks, k, EDGE), BF16),
        in_specs=[VMEM_SPEC, VMEM_SPEC],
        out_specs=VMEM_SPEC,
        scratch_shapes=[
            VMEM((bands, share, k, EDGE), F32), VMEM((share, k, EDGE), BF16),
            DMA((bands,)), DMA((bands,)), DMA((bands,)), DMA((bands,)),
        ],
        compiler_params=params(2),
        name="sum_bands",
    )(forward, obs_weight.reshape(row_blocks, 1, EDGE))

    part = pl.pallas_call(
        functools.partial(adjoint_kernel, per_step),
        grid=(blocks // per_step,),
        out_shape=jax.ShapeDtypeStruct((k * field_rows, EDGE), F32),
        in_specs=smem + [pl.BlockSpec((row_blocks, k, EDGE), lambda i: (0, 0, 0)), block_spec],
        out_specs=pl.BlockSpec((k * field_rows, EDGE), lambda i: (0, 0)),
        compiler_params=params(),
        name="adjoint",
    )(rows, cols, scale, values, footprints)

    half = (HALF, EDGE)
    change = pl.pallas_call(
        functools.partial(image_kernel, sizes),
        out_shape=jax.ShapeDtypeStruct((k, *field), WIRE_IMAGE),
        in_specs=[ANY_SPEC, VMEM_SPEC],
        out_specs=ANY_SPEC,
        scratch_shapes=[
            VMEM((CHIPS, *field), F32), VMEM((CHIPS, *field), F32), VMEM((CHIPS, *field), WIRE_SUM),
            VMEM((2, *half), WIRE_SUM), VMEM((2, *field), WIRE_SUM), VMEM(field, WIRE_BACK), VMEM((2, *field), WIRE_BACK),
            VMEM(field, WIRE_IMAGE),
            DMA((9,)), DMA((9,)), DMA((2,)), DMA((2,)), DMA((CHIPS,)), DMA((CHIPS,)), DMA((CHIPS,)), DMA((CHIPS,)),
            DMA((CHIPS,)), DMA(()),
        ],
        compiler_params=params(3),
        name="image",
    )(part.reshape(k, *field), widths)

    change = change.reshape(k, lon_blocks, EDGE, EDGE)
    native = pl.BlockSpec((k, 1, band_rows, nlon), lambda w: (0, w, 0, 0))
    packed = pl.BlockSpec((k, lon_blocks, band_rows, EDGE), lambda w: (0, 0, w, 0))
    gram = pl.pallas_call(
        functools.partial(gram_kernel, k),
        grid=(weeks,),
        out_shape=jax.ShapeDtypeStruct((k, EDGE), F32),
        in_specs=[native, native, packed],
        out_specs=pl.BlockSpec((k, EDGE), lambda w: (0, 0)),
        scratch_shapes=[VMEM((4, k, k, 8, EDGE), F32)],
        compiler_params=params(),
        name="gram",
    )(residual, direction, change)

    coef = pl.pallas_call(
        functools.partial(solve_kernel, bands),
        out_shape=jax.ShapeDtypeStruct((k, EDGE), F32),
        in_specs=[VMEM_SPEC],
        out_specs=VMEM_SPEC,
        scratch_shapes=[VMEM((bands, k, EDGE), F32), DMA((bands,)), DMA((bands,))],
        compiler_params=params(4),
        name="solve",
    )(gram)

    return pl.pallas_call(
        functools.partial(update_kernel, k),
        grid=(weeks,),
        out_shape=[jax.ShapeDtypeStruct(direction.shape, F32)] * 3,
        in_specs=[SMEM_SPEC, native, native, native, packed],
        out_specs=[native] * 3,
        compiler_params=params(),
        name="update",
    )(coef, solution, residual, direction, change)


def solution(mesh):
    assert mesh.shape["obs"] == 2 * CHIPS
    three = (P(None, None, "lat", None),) * 3
    blocks = P("obs", "lat", None)
    return jax.shard_map(
        functools.partial(shards, mesh.shape["lat"]),
        mesh=mesh,
        in_specs=(P("obs", "lat", None, None, None), blocks, blocks, blocks, P(), P(), P("obs"), *three),
        out_specs=three,
        check_vma=False,
    )
```

```python
import functools

import jax
import jax.numpy as jnp
from jax import lax
from jax.experimental import pallas as pl
from jax.experimental.pallas import tpu as pltpu
from jax.sharding import PartitionSpec as P

MESH = pl.DeviceIdType.MESH
HIGHEST = lax.Precision.HIGHEST
F32 = jnp.float32
BF16 = jnp.bfloat16
VMEM = pltpu.VMEM
DMA = pltpu.SemaphoreType.DMA
EDGE = 128
CHIPS = 4
ANY_SPEC = pl.BlockSpec(memory_space=pl.ANY)
VMEM_SPEC = pl.BlockSpec(memory_space=pltpu.VMEM)
SMEM_SPEC = pl.BlockSpec(memory_space=pltpu.SMEM)
BAND = 32
WEEK = 160
CODED = WEEK + 16
FIELD = 640
STEP = FIELD + 1
TOP = 32000.0


def iota(shape, axis):
    return lax.broadcasted_iota(jnp.int32, shape, axis)


def norm_of(width, decay):
    p = jnp.exp(jnp.full_like(width, -2.0 / decay))
    return jnp.sqrt(1.0 + 2.0 * p * (1.0 - jnp.exp(width * (-2.0 / decay))) / (1.0 - p))


def down_rows(row):
    return jnp.transpose(jnp.broadcast_to(row, (EDGE, EDGE)))


def along_lon(blocks, width, decay, bits):
    rows = blocks[0].shape[0]
    count = len(blocks)
    lane = iota((rows, EDGE), 1)
    terms = width.astype(jnp.int32) + 1
    picks = [((terms >> m) & 1) == 1 for m in range(bits)]

    def shifted(values, step, sign):
        turned = [pltpu.roll(v, step if sign > 0 else EDGE - step, 1) for v in values]
        inside = lane >= step if sign > 0 else lane < EDGE - step
        return [jnp.where(inside, turned[b], turned[(b - sign) % count]) for b in range(count)]

    sides = []
    for sign in (1, -1):
        power = blocks
        total = [jnp.where(picks[0], v, 0.0) for v in blocks]
        for m in range(1, bits):
            half = 2 ** (m - 1)
            moved = shifted(power, half, sign)
            fade = jnp.exp(jnp.full((rows, EDGE), -half / decay, F32))
            power = [a + fade * c for a, c in zip(power, moved)]
            moved = shifted(total, 2 * half, sign)
            fade = fade * fade
            total = [jnp.where(picks[m], a + fade * c, t) for a, c, t in zip(power, moved, total)]
        sides.append(total)
    scale = 1.0 / norm_of(width, decay)
    return [(up + down - x) * scale for up, down, x in zip(sides[0], sides[1], blocks)]


def lat_rows(widths, reach, l, bands, across):
    r, c = iota((BAND, EDGE), 0), iota((BAND, EDGE), 1)
    width = widths[1:2, :] if across else down_rows(widths[1:2, :])[BAND:2 * BAND]
    distance = jnp.abs(r - c + BAND).astype(F32)
    low = jnp.where(l > 0, 0, BAND)
    high = jnp.where(l < bands - 1, 3 * BAND, 2 * BAND)
    value = jnp.exp(-distance / reach) / norm_of(width, reach)
    return jnp.where((distance <= width) & (c >= low) & (c < high), value, 0.0)


def mix_rows(weights, stacks):
    weights = weights[:, :3 * BAND]
    large = weights.astype(BF16)
    both = jnp.concatenate([large, (weights - large.astype(F32)).astype(BF16)], axis=0)
    stack = jnp.concatenate(stacks, axis=1)
    first = stack.astype(BF16)
    second = (stack - first.astype(F32)).astype(BF16)
    main = jnp.dot(both, first, preferred_element_type=F32)
    total = main[:BAND] + (main[BAND:] + jnp.dot(large, second, preferred_element_type=F32))
    return [total[:, b * EDGE:(b + 1) * EDGE] for b in range(len(stacks))]


def encode(ref, blocks):
    row = iota((16, EDGE), 0)
    powers = jnp.zeros((16, EDGE), F32)
    for b, value in enumerate(blocks):
        top = jnp.max(jnp.abs(value), axis=0, keepdims=True)
        power = jnp.ceil(jnp.log2(jnp.maximum(top, 1e-30)))
        whole = jnp.round(value * (jnp.exp2(-power) * TOP))
        ref[b * BAND:(b + 1) * BAND, :] = whole.astype(jnp.int32).astype(jnp.int16)
        powers = jnp.where(row == b, jnp.broadcast_to(power, (16, EDGE)), powers)
    ref[WEEK:CODED, :] = powers.astype(jnp.int32).astype(jnp.int16)


def scales_of(ref, count):
    powers = jnp.exp2(ref[WEEK:CODED, :].astype(jnp.int32).astype(F32)) * (1.0 / TOP)
    return [powers[b:b + 1, :] for b in range(count)]


def decode(ref, count):
    scales = scales_of(ref, count)
    return [ref[b * BAND:(b + 1) * BAND, :].astype(jnp.int32).astype(F32) * scales[b] for b in range(count)]


def greet(peers):
    barrier = pltpu.get_barrier_semaphore()
    for peer in peers:
        pl.semaphore_signal(barrier, inc=1, device_id=peer, device_id_type=MESH)
    pl.semaphore_wait(barrier, len(peers))


def obs_peers(o):
    z, c = o // 2, o % 2

    def at(step, core):
        return ((z + step + CHIPS) % CHIPS) * 2 + core

    return z, c, at


def remote(src, dst, sems, at, to):
    send, recv = sems
    return pltpu.make_async_remote_copy(
        src_ref=src, dst_ref=dst, send_sem=send.at[at], recv_sem=recv.at[at], device_id=to, device_id_type=MESH,
    )


class Gather:
    def __init__(self, own_ref, out_ref, o, sems, local):
        self.own, self.out, self.o, self.sems = own_ref, out_ref, o, sems
        self.z, self.c, self.at = obs_peers(o)
        self.partner, self.up, self.down = ({"obs": self.at(*p)} for p in ((0, 1 - self.c), (1, self.c), (-1, self.c)))
        self.weeks = own_ref.shape[0]
        self.keep = [pltpu.make_async_copy(own_ref.at[w], out_ref.at[o, w], local.at[w]) for w in range(self.weeks)]
        self.started = []

    def copy(self, role, w, step, core, to):
        ref = self.out.at[self.at(step, core), w]
        return remote(self.own.at[w] if role < 3 else ref, self.out.at[self.o, w] if role < 3 else ref, self.sems, (role, w), to)

    def arrival(self, role, w, step, core):
        ref = self.out.at[self.at(step, core), w]
        remote(self.own.at[w], ref, self.sems, (role, w), self.partner).wait_recv()

    def start(self, *copies):
        for one in copies:
            one.start()
        self.started += copies

    def far_way(self, w):
        return (3, -1, self.up) if w < 2 else (3, 1, self.down)

    def send(self, w):
        self.start(self.copy(1, w, 0, self.c, self.up), self.copy(2, w, 0, self.c, self.down), self.copy(0, w, 0, self.c, self.partner))
        self.keep[w].start()

    def forward(self, w):
        for role, step in ((1, -1), (2, 1)) if w < 2 else ((2, 1), (1, -1)):
            self.arrival(role, w, step, self.c)
            far, far_step, way = self.far_way(w)
            if step == far_step:
                self.start(self.copy(far, w, step, self.c, way))
            self.start(self.copy(3 + role, w, step, self.c, self.partner))

    def relay(self, w):
        self.arrival(3, w, 2, self.c)
        self.start(self.copy(6, w, 2, self.c, self.partner))

    def finish(self):
        for w in range(self.weeks):
            for role, step in ((0, 0), (4, -1), (5, 1), (6, 2)):
                self.arrival(role, w, step, 1 - self.c)
        for one in self.started:
            one.wait_send()
        for one in self.keep:
            one.wait()


def run_gather(gather, order, produce):
    for n, w in enumerate(order):
        produce(w)
        gather.send(w)
        if n >= 1:
            gather.forward(order[n - 1])
        if n >= 2:
            gather.relay(order[n - 2])
    gather.forward(order[-1])
    gather.relay(order[-2])
    gather.relay(order[-1])
    gather.finish()


def halo_copies(src_ref, halo_ref, w, l, bands, sems):
    return [
        remote(src_ref.at[w], halo_ref.at[slot, w], sems, (slot, w), {"lat": (l + step) % bands})
        for slot, step in ((0, 1), (1, bands - 1))
    ]


def stacks_of(low, mid, high):
    return [jnp.concatenate(three, axis=0) for three in zip(low, mid, high)]


def blocks_of(ref, count):
    return [ref[b * BAND:(b + 1) * BAND, :] for b in range(count)]


def put_blocks(ref, blocks):
    for b, value in enumerate(blocks):
        ref[b * BAND:(b + 1) * BAND, :] = value.astype(ref.dtype)


def spread_kernel(sizes, direction_ref, widths_ref, out_ref, field, smooth, wire, halo, shard, send, recv, hsend, hrecv, load, local):
    o, l = lax.axis_index("obs"), lax.axis_index("lat")
    bands, weeks, count, bits, lat_decay, lon_decay = sizes
    loads = [pltpu.make_async_copy(direction_ref.at[o, w], field.at[w], load.at[w]) for w in range(weeks)]
    for one in loads:
        one.start()
    z, c, at = obs_peers(o)
    greet([{"obs": at(0, 1 - c)}, {"obs": at(1, c)}, {"obs": at(-1, c)},
           {"lat": (l + 1) % bands}, {"lat": (l + bands - 1) % bands}])
    lon_width = down_rows(widths_ref[0:1, :])[0:BAND]
    weights = lat_rows(widths_ref, lat_decay, l, bands, False)
    halos = []

    def begin(w):
        loads[w].wait()
        done = along_lon([field[w, :, b * EDGE:(b + 1) * EDGE] for b in range(count)], lon_width, lon_decay, bits)
        encode(wire.at[w], done)
        halos.append(halo_copies(wire, halo, w, l, bands, (hsend, hrecv)))
        for one in halos[w]:
            one.start()
        put_blocks(smooth.at[w], done)

    begin(0)
    begin(1)

    def produce(w):
        if w + 2 < weeks:
            begin(w + 2)
        for one in halos[w]:
            one.wait_recv()
        stacks = stacks_of(decode(halo.at[0, w], count), blocks_of(smooth.at[w], count), decode(halo.at[1, w], count))
        put_blocks(shard.at[w], mix_rows(weights, stacks))

    run_gather(Gather(shard, out_ref, o, (send, recv), local), range(weeks), produce)
    for pair_of in halos:
        for one in pair_of:
            one.wait_send()


def pair(first, second):
    none = jnp.zeros_like(first)
    return jnp.concatenate([jnp.concatenate([first, none], axis=1), jnp.concatenate([none, second], axis=1)], axis=0)


def place_of(col):
    row = (col * 6554) >> 15
    return pl.ds((row >> 5) * WEEK + (col - 5 * row) * BAND + (row & 31), 8, stride=STEP)


def factor_of(scale):
    return (8 >> scale).astype(F32) * 0.125


def forward_kernel(per_step, rows_ref, cols_ref, scale_ref, cells_ref, blocks_ref, out_ref, cells):
    step = pl.program_id(0)

    @pl.when(step == 0)
    def _():
        for k in range(8):
            cells[k * STEP:k * STEP + FIELD, :] = cells_ref[k * FIELD:(k + 1) * FIELD, :].astype(F32)
        out_ref[...] = jnp.zeros_like(out_ref)

    def two(n, carry):
        at = [step * per_step + 2 * n + i for i in range(2)]
        picked = pair(*[cells[place_of(cols_ref[0, 0, a]), :].astype(BF16) for a in at])
        both = jnp.concatenate([blocks_ref[2 * n], blocks_ref[2 * n + 1]], axis=1)
        value = lax.dot_general(picked, both, (((1,), (1,)), ((), ())), preferred_element_type=F32)
        for i, a in enumerate(at):
            row = rows_ref[0, 0, a]
            out_ref[row] = out_ref[row] + value[8 * i:8 * i + 8] * factor_of(scale_ref[0, 0, a])
        return carry

    lax.fori_loop(0, per_step // 2, two, 0, unroll=8)


def adjoint_kernel(per_step, rows_ref, cols_ref, scale_ref, values_ref, blocks_ref, out_ref, total):
    step = pl.program_id(0)

    @pl.when(step == 0)
    def _():
        total[...] = jnp.zeros_like(total)

    def two(n, carry):
        at = [step * per_step + 2 * n + i for i in range(2)]
        pulled = jnp.concatenate([values_ref[rows_ref[0, 0, a]] for a in at], axis=0)
        both = jnp.concatenate([blocks_ref[2 * n], blocks_ref[2 * n + 1]], axis=1)
        value = jnp.dot(pulled, both, preferred_element_type=F32)
        for i, a in enumerate(at):
            place = place_of(cols_ref[0, 0, a])
            part = value[8 * i:8 * i + 8, EDGE * i:EDGE * i + EDGE]
            total[place, :] = total[place, :] + part * factor_of(scale_ref[0, 0, a])
        return carry

    lax.fori_loop(0, per_step // 2, two, 0, unroll=8)

    @pl.when(step == pl.num_programs(0) - 1)
    def _():
        for k in range(8):
            out_ref[k * FIELD:(k + 1) * FIELD, :] = total[k * STEP:k * STEP + FIELD, :]


def sum_bands_kernel(bands, part_ref, weight_ref, out_ref, got, shard, send, recv, send2, recv2):
    l = lax.axis_index("lat")
    share = part_ref.shape[0] // bands
    greet([{"lat": (l + d) % bands} for d in range(1, bands)])
    mine = pl.ds(l * share, share)

    def first(d):
        peer = (l + d) % bands
        return pltpu.make_async_remote_copy(
            src_ref=part_ref.at[pl.ds(peer * share, share)], dst_ref=got.at[d], send_sem=send.at[d], recv_sem=recv.at[d],
            device_id={"lat": peer}, device_id_type=MESH,
        )

    def second(d, owner):
        return pltpu.make_async_remote_copy(
            src_ref=shard, dst_ref=out_ref.at[pl.ds(owner * share, share)], send_sem=send2.at[d], recv_sem=recv2.at[d],
            device_id={"lat": (l + d) % bands}, device_id_type=MESH,
        )

    for d in range(1, bands):
        first(d).start()
    total = part_ref[mine]
    for d in range(1, bands):
        first(d).wait_recv()
        total = total + got[d]
    weight = weight_ref[mine]
    shard[...] = (total * weight).astype(shard.dtype)
    for d in range(1, bands):
        second(d, l).start()
    out_ref[mine] = shard[...]
    for d in range(1, bands):
        second(d, (l + bands - d) % bands).wait_recv()
    for d in range(1, bands):
        first(d).wait_send()
        second(d, l).wait_send()


def image_kernel(sizes, part_ref, widths_ref, out_ref, own, there, far_out, near_out, relay_out, far_in, near_in, relay_in,
                 mine, band, halo, shard, send, recv, hsend, hrecv, psend, precv, rsend, rrecv, load, local):
    o, l = lax.axis_index("obs"), lax.axis_index("lat")
    bands, weeks, count, bits, lat_decay, lon_decay = sizes
    z, c, at = obs_peers(o)
    partner, up, down = {"obs": at(0, 1 - c)}, {"obs": at(1, c)}, {"obs": at(-1, c)}
    greet([partner, up, down, {"lat": (l + 1) % bands}, {"lat": (l + bands - 1) % bands}])
    order = (0, 2, 1, 3)

    def rows_for(core, w):
        return part_ref.at[:, core, w]

    swaps = [remote(rows_for(1 - c, w), there.at[w], (psend, precv), w, partner) for w in range(weeks)]
    loads = [pltpu.make_async_copy(rows_for(c, w), own.at[w], load.at[w]) for w in range(weeks)]
    for w in order:
        swaps[w].start()
        loads[w].start()
    lon_width = down_rows(widths_ref[0:1, :])[0:BAND]
    weights = lat_rows(widths_ref, lat_decay, l, bands, True)
    ring = (rsend, rrecv)

    def way(w):
        return (1, up, down) if w < 2 else (-1, down, up)

    far = [remote(far_out.at[w], far_in.at[w], ring, (0, w), way(w)[1]) for w in range(weeks)]
    relayed = [remote(relay_out.at[w], relay_in.at[w], ring, (1, w), way(w)[1]) for w in range(weeks)]
    near = [remote(near_out.at[w], near_in.at[w], ring, (2, w), way(w)[2]) for w in range(weeks)]
    halos = [halo_copies(band, halo, w, l, bands, (hsend, hrecv)) for w in range(weeks)]

    def chip_sum(w, step):
        there_too = (z + step + CHIPS) % CHIPS
        return [x + y for x, y in zip(blocks_of(own.at[w, there_too], count), blocks_of(there.at[w, there_too], count))]

    def plus(x, y):
        return [a + d for a, d in zip(x, y)]

    for w in order:
        swaps[w].wait_recv()
        loads[w].wait()
        encode(far_out.at[w], chip_sum(w, 2))
        far[w].start()
        encode(near_out.at[w], chip_sum(w, -way(w)[0]))
        near[w].start()
    for w in order:
        far[w].wait_recv()
        encode(relay_out.at[w], plus(chip_sum(w, way(w)[0]), decode(far_in.at[w], count)))
        relayed[w].start()
    for w in order:
        near[w].wait_recv()
        relayed[w].wait_recv()
        total = plus(plus(chip_sum(w, 0), decode(near_in.at[w], count)), decode(relay_in.at[w], count))
        encode(band.at[w], total)
        for one in halos[w]:
            one.start()
        put_blocks(mine.at[w], total)

    def produce(w):
        for one in halos[w]:
            one.wait_recv()
        stacks = stacks_of(decode(halo.at[0, w], count), blocks_of(mine.at[w], count), decode(halo.at[1, w], count))
        encode(shard.at[w], along_lon(mix_rows(weights, stacks), lon_width, lon_decay, bits))

    run_gather(Gather(shard, out_ref, o, (send, recv), local), order, produce)
    for w in range(weeks):
        for one in (swaps[w], far[w], relayed[w], near[w], *halos[w]):
            one.wait_send()


def change_block(change_ref, i, b, first, rows):
    at = b * BAND + first
    at = at if isinstance(at, int) else pl.multiple_of(at, 16)
    power = change_ref[i, 0, WEEK:CODED, :].astype(jnp.int32).astype(F32)
    pick = jnp.sum(jnp.where(iota((16, EDGE), 0) == b, power, 0.0), axis=0, keepdims=True)
    return change_ref[i, 0, pl.ds(at, rows), :].astype(jnp.int32).astype(F32) * (jnp.exp2(pick) * (1.0 / TOP))


def gram_kernel(k, residual_ref, direction_ref, change_ref, out_ref, sums):
    step = pl.program_id(0)
    lon_blocks = 5

    @pl.when(step == 0)
    def _():
        sums[...] = jnp.zeros_like(sums)

    def one(b, carry):
        lanes = pl.ds(pl.multiple_of(b * EDGE, EDGE), EDGE)
        res = [residual_ref[i, 0, :, lanes] for i in range(k)]
        dire = [direction_ref[i, 0, :, lanes] for i in range(k)]
        img = [dire[i] + change_block(change_ref, i, b, 0, BAND) for i in range(k)]

        def add(t, i, j, x, y):
            sums[t, i, j] = sums[t, i, j] + jnp.sum((x * y).reshape(4, 8, EDGE), axis=0)

        for i in range(k):
            for j in range(k):
                if i <= j:
                    add(0, i, j, res[i], res[j])
                    add(3, i, j, img[i], img[j])
                add(1, i, j, dire[i], img[j])
                add(2, i, j, img[i], res[j])
        return carry

    lax.fori_loop(0, lon_blocks, one, 0)

    @pl.when(step == pl.num_programs(0) - 1)
    def _():
        lane, row = iota((k, EDGE), 1), iota((k, EDGE), 0)
        result = jnp.zeros((k, EDGE), F32)
        for t in range(4):
            for i in range(k):
                line = jnp.sum(jnp.sum(sums[t, i], axis=1), axis=1, keepdims=True)
                line = jnp.broadcast_to(line, (k, EDGE))
                result = jnp.where(lane == t * k + i, line, result)
        out_ref[...] = result


def flip(x):
    square = jnp.concatenate([x, jnp.zeros((EDGE - 8, EDGE), F32)], axis=0)
    return jnp.transpose(square)[:8, :]


def product(x, y):
    return sum(jnp.broadcast_to(x[:, i:i + 1], (8, EDGE)) * jnp.broadcast_to(y[i:i + 1, :], (8, EDGE)) for i in range(8))


def solve(a, b):
    row = iota((8, EDGE), 0)
    for p in range(8):
        line = jnp.broadcast_to(a[p:p + 1, :], (8, EDGE))
        line_b = jnp.broadcast_to(b[p:p + 1, :], (8, EDGE))
        column = jnp.broadcast_to(a[:, p:p + 1], (8, EDGE))
        inverse = 1.0 / jnp.broadcast_to(a[p:p + 1, p:p + 1], (8, EDGE))
        ratio = column * inverse
        here = row == p
        a = jnp.where(here, line * inverse, a - ratio * line)
        b = jnp.where(here, line_b * inverse, b - ratio * line_b)
    return b


def solve_kernel(bands, part_ref, out_ref, got, send, recv):
    l = lax.axis_index("lat")
    greet([{"lat": (l + d) % bands} for d in range(1, bands)])

    def to(d):
        return pltpu.make_async_remote_copy(
            src_ref=part_ref, dst_ref=got.at[l], send_sem=send.at[d], recv_sem=recv.at[d],
            device_id={"lat": (l + d) % bands}, device_id_type=MESH,
        )

    for d in range(1, bands):
        to(d).start()
    got[l] = part_ref[...]
    for d in range(1, bands):
        to(d).wait_recv()
    total = got[0]
    for d in range(1, bands):
        total = total + got[d]
    lane, row = iota((8, EDGE), 1), iota((8, EDGE), 0)
    parts = []
    for t in range(4):
        moved = total if t == 0 else pltpu.roll(total, EDGE - 8 * t, 1)
        parts.append(jnp.where(lane < 8, moved, 0.0))

    def full(x):
        low = jnp.where(lane <= row, x, 0.0)
        return low + flip(jnp.where(lane < row, x, 0.0))

    gram_old, image_image = full(parts[0]), full(parts[3])
    curvature = 0.5 * (parts[1] + flip(parts[1]))
    residual_image = parts[2]
    step = solve(curvature, gram_old)
    cross = product(residual_image, step)
    gram_new = gram_old - cross - flip(cross) + product(flip(step), product(image_image, step))
    turn = solve(gram_old, gram_new)
    out_ref[...] = jnp.where(lane < 8, step, 0.0) + pltpu.roll(jnp.where(lane < 8, turn, 0.0), 8, 1)
    for d in range(1, bands):
        to(d).wait_send()


def update_kernel(k, coef_ref, solution_ref, residual_ref, direction_ref, change_ref, sol_out, res_out, dir_out):
    rows_each = 32

    def one(b, carry):
        lanes = pl.ds(pl.multiple_of(b * EDGE, EDGE), EDGE)
        for r in range(BAND // rows_each):
            rows = slice(r * rows_each, (r + 1) * rows_each)
            dire = [direction_ref[i, 0, rows, lanes] for i in range(k)]
            more = [change_block(change_ref, i, b, r * rows_each, rows_each) for i in range(k)]
            for a in range(k):
                forth = sum(coef_ref[i, a] * dire[i] for i in range(k))
                back = sum(coef_ref[i, a] * more[i] for i in range(k))
                turn = sum(coef_ref[i, k + a] * dire[i] for i in range(k))
                left = residual_ref[a, 0, rows, lanes] - (forth + back)
                sol_out[a, 0, rows, lanes] = solution_ref[a, 0, rows, lanes] + forth
                res_out[a, 0, rows, lanes] = left
                dir_out[a, 0, rows, lanes] = left + turn
        return carry

    lax.fori_loop(0, 5, one, 0)


def params(collective=None, limit=None):
    extra = {} if collective is None else {"collective_id": collective, "has_side_effects": True}
    return pltpu.CompilerParams(vmem_limit_bytes=limit or (48 << 20), **extra)


def shards(bands, footprints, block_rows, block_cols, block_scale, lat_width, lon_width, obs_weight, solution, residual, direction):
    k, weeks, band_rows, nlon = direction.shape
    blocks = footprints.shape[2]
    count = nlon // EDGE
    assert (k, weeks, band_rows, count) == (8, 4, BAND, 5)
    row_blocks = obs_weight.shape[0] // EDGE
    sizes = (bands, weeks, count, (nlon // 8 + 1).bit_length(), band_rows / 2.0, nlon / 32.0)
    l = lax.axis_index("lat")
    lon_own = lax.dynamic_slice_in_dim(lon_width, l * BAND, BAND)
    lat_near = lax.dynamic_slice_in_dim(jnp.pad(lat_width, BAND), l * BAND, 3 * BAND)
    widths = jnp.pad(jnp.stack([jnp.pad(lon_own, (0, 3 * BAND)), jnp.pad(lat_near, (0, BAND))]), ((0, 6), (0, 0))).astype(F32)
    all_rows = k * weeks * WEEK
    plain, coded = (weeks, WEEK, EDGE), (weeks, CODED, EDGE)
    ints = jnp.int16

    cells = pl.pallas_call(
        functools.partial(spread_kernel, sizes),
        out_shape=jax.ShapeDtypeStruct((k, *plain), BF16),
        in_specs=[ANY_SPEC, VMEM_SPEC],
        out_specs=ANY_SPEC,
        scratch_shapes=[
            VMEM((weeks, band_rows, nlon), F32), VMEM(plain, F32), VMEM(coded, ints), VMEM((2, *coded), ints), VMEM(plain, BF16),
            DMA((7, weeks)), DMA((7, weeks)), DMA((2, weeks)), DMA((2, weeks)), DMA((weeks,)), DMA((weeks,)),
        ],
        compiler_params=params(1, 65_000_000),
        name="spread",
    )(direction, widths)

    per_step = 48
    smem = [SMEM_SPEC] * 3
    block_spec = pl.BlockSpec((None, None, per_step, EDGE, EDGE), lambda i: (0, 0, i, 0, 0))
    forward = pl.pallas_call(
        functools.partial(forward_kernel, per_step),
        grid=(blocks // per_step,),
        out_shape=jax.ShapeDtypeStruct((row_blocks, k, EDGE), F32),
        in_specs=smem + [pl.BlockSpec((all_rows, EDGE), lambda i: (0, 0)), block_spec],
        out_specs=pl.BlockSpec((row_blocks, k, EDGE), lambda i: (0, 0, 0)),
        scratch_shapes=[VMEM((k * STEP, EDGE), F32)],
        compiler_params=params(),
        name="forward",
    )(block_rows, block_cols, block_scale, cells.reshape(all_rows, EDGE), footprints)

    share = row_blocks // bands
    values = pl.pallas_call(
        functools.partial(sum_bands_kernel, bands),
        out_shape=jax.ShapeDtypeStruct((row_blocks, k, EDGE), BF16),
        in_specs=[VMEM_SPEC, VMEM_SPEC],
        out_specs=VMEM_SPEC,
        scratch_shapes=[
            VMEM((bands, share, k, EDGE), F32), VMEM((share, k, EDGE), BF16),
            DMA((bands,)), DMA((bands,)), DMA((bands,)), DMA((bands,)),
        ],
        compiler_params=params(2),
        name="sum_bands",
    )(forward, obs_weight.reshape(row_blocks, 1, EDGE))

    part = pl.pallas_call(
        functools.partial(adjoint_kernel, per_step),
        grid=(blocks // per_step,),
        out_shape=jax.ShapeDtypeStruct((all_rows, EDGE), F32),
        in_specs=smem + [pl.BlockSpec((row_blocks, k, EDGE), lambda i: (0, 0, 0)), block_spec],
        out_specs=pl.BlockSpec((all_rows, EDGE), lambda i: (0, 0)),
        scratch_shapes=[VMEM((k * STEP, EDGE), F32)],
        compiler_params=params(),
        name="adjoint",
    )(block_rows, block_cols, block_scale, values, footprints)

    change = pl.pallas_call(
        functools.partial(image_kernel, sizes),
        out_shape=jax.ShapeDtypeStruct((k, *coded), ints),
        in_specs=[ANY_SPEC, VMEM_SPEC],
        out_specs=ANY_SPEC,
        scratch_shapes=[
            VMEM((weeks, CHIPS, WEEK, EDGE), F32), VMEM((weeks, CHIPS, WEEK, EDGE), F32),
            *[VMEM(coded, ints)] * 6, VMEM(plain, F32), VMEM(coded, ints), VMEM((2, *coded), ints), VMEM(coded, ints),
            DMA((7, weeks)), DMA((7, weeks)), DMA((2, weeks)), DMA((2, weeks)), DMA((weeks,)), DMA((weeks,)),
            DMA((3, weeks)), DMA((3, weeks)), DMA((weeks,)), DMA((weeks,)),
        ],
        compiler_params=params(3),
        name="image",
    )(part.reshape(CHIPS, 2, *plain), widths)

    native = pl.BlockSpec((k, 1, band_rows, nlon), lambda w: (0, w, 0, 0))
    packed = pl.BlockSpec((k, 1, CODED, EDGE), lambda w: (0, w, 0, 0))
    gram = pl.pallas_call(
        functools.partial(gram_kernel, k),
        grid=(weeks,),
        out_shape=jax.ShapeDtypeStruct((k, EDGE), F32),
        in_specs=[native, native, packed],
        out_specs=pl.BlockSpec((k, EDGE), lambda w: (0, 0)),
        scratch_shapes=[VMEM((4, k, k, 8, EDGE), F32)],
        compiler_params=params(),
        name="gram",
    )(residual, direction, change)

    coef = pl.pallas_call(
        functools.partial(solve_kernel, bands),
        out_shape=jax.ShapeDtypeStruct((k, EDGE), F32),
        in_specs=[VMEM_SPEC],
        out_specs=VMEM_SPEC,
        scratch_shapes=[VMEM((bands, k, EDGE), F32), DMA((bands,)), DMA((bands,))],
        compiler_params=params(4),
        name="solve",
    )(gram)

    return pl.pallas_call(
        functools.partial(update_kernel, k),
        grid=(weeks,),
        out_shape=[jax.ShapeDtypeStruct(direction.shape, F32)] * 3,
        in_specs=[SMEM_SPEC, native, native, native, packed],
        out_specs=[native] * 3,
        compiler_params=params(),
        name="update",
    )(coef, solution, residual, direction, change)


def solution(mesh):
    assert mesh.shape["obs"] == 2 * CHIPS
    three = (P(None, None, "lat", None),) * 3
    blocks = P("obs", "lat", None)
    return jax.shard_map(
        functools.partial(shards, mesh.shape["lat"]),
        mesh=mesh,
        in_specs=(P("obs", "lat", None, None, None), blocks, blocks, blocks, P(), P(), P("obs"), *three),
        out_specs=three,
        check_vma=False,
    )
```

```python
import functools

import jax
import jax.numpy as jnp
from jax import lax
from jax.experimental import pallas as pl
from jax.experimental.pallas import tpu as pltpu
from jax.sharding import PartitionSpec as P

MESH = pl.DeviceIdType.MESH
HIGHEST = lax.Precision.HIGHEST
F32 = jnp.float32
BF16 = jnp.bfloat16
VMEM = pltpu.VMEM
DMA = pltpu.SemaphoreType.DMA
EDGE = 128
CHIPS = 4
ANY_SPEC = pl.BlockSpec(memory_space=pl.ANY)
VMEM_SPEC = pl.BlockSpec(memory_space=pltpu.VMEM)
SMEM_SPEC = pl.BlockSpec(memory_space=pltpu.SMEM)
BAND = 32
WEEK = 160
CODED = WEEK + 16
FIELD = 640
STEP = FIELD + 1
TOP = 32000.0


def iota(shape, axis):
    return lax.broadcasted_iota(jnp.int32, shape, axis)


def norm_of(width, decay):
    p = jnp.exp(jnp.full_like(width, -2.0 / decay))
    return jnp.sqrt(1.0 + 2.0 * p * (1.0 - jnp.exp(width * (-2.0 / decay))) / (1.0 - p))


def down_rows(row):
    return jnp.transpose(jnp.broadcast_to(row, (EDGE, EDGE)))


def along_lon(blocks, width, decay, bits):
    rows = blocks[0].shape[0]
    count = len(blocks)
    lane = iota((rows, EDGE), 1)
    terms = width.astype(jnp.int32) + 1
    picks = [((terms >> m) & 1) == 1 for m in range(bits)]

    def shifted(values, step, sign):
        turned = [pltpu.roll(v, step if sign > 0 else EDGE - step, 1) for v in values]
        inside = lane >= step if sign > 0 else lane < EDGE - step
        return [jnp.where(inside, turned[b], turned[(b - sign) % count]) for b in range(count)]

    sides = []
    for sign in (1, -1):
        power = blocks
        total = [jnp.where(picks[0], v, 0.0) for v in blocks]
        for m in range(1, bits):
            half = 2 ** (m - 1)
            moved = shifted(power, half, sign)
            fade = jnp.exp(jnp.full((rows, EDGE), -half / decay, F32))
            power = [a + fade * c for a, c in zip(power, moved)]
            moved = shifted(total, 2 * half, sign)
            fade = fade * fade
            total = [jnp.where(picks[m], a + fade * c, t) for a, c, t in zip(power, moved, total)]
        sides.append(total)
    scale = 1.0 / norm_of(width, decay)
    return [(up + down - x) * scale for up, down, x in zip(sides[0], sides[1], blocks)]


def lat_rows(widths, reach, l, bands, across):
    r, c = iota((BAND, EDGE), 0), iota((BAND, EDGE), 1)
    width = widths[1:2, :] if across else down_rows(widths[1:2, :])[BAND:2 * BAND]
    distance = jnp.abs(r - c + BAND).astype(F32)
    low = jnp.where(l > 0, 0, BAND)
    high = jnp.where(l < bands - 1, 3 * BAND, 2 * BAND)
    value = jnp.exp(-distance / reach) / norm_of(width, reach)
    return jnp.where((distance <= width) & (c >= low) & (c < high), value, 0.0)


def mix_rows(weights, stacks):
    weights = weights[:, :3 * BAND]
    large = weights.astype(BF16)
    both = jnp.concatenate([large, (weights - large.astype(F32)).astype(BF16)], axis=0)
    stack = jnp.concatenate(stacks, axis=1)
    first = stack.astype(BF16)
    second = (stack - first.astype(F32)).astype(BF16)
    main = jnp.dot(both, first, preferred_element_type=F32)
    total = main[:BAND] + (main[BAND:] + jnp.dot(large, second, preferred_element_type=F32))
    return [total[:, b * EDGE:(b + 1) * EDGE] for b in range(len(stacks))]


def encode(ref, blocks):
    row = iota((16, EDGE), 0)
    powers = jnp.zeros((16, EDGE), F32)
    for b, value in enumerate(blocks):
        top = jnp.max(jnp.abs(value), axis=0, keepdims=True)
        power = jnp.ceil(jnp.log2(jnp.maximum(top, 1e-30)))
        whole = jnp.round(value * (jnp.exp2(-power) * TOP))
        ref[b * BAND:(b + 1) * BAND, :] = whole.astype(jnp.int32).astype(jnp.int16)
        powers = jnp.where(row == b, jnp.broadcast_to(power, (16, EDGE)), powers)
    ref[WEEK:CODED, :] = powers.astype(jnp.int32).astype(jnp.int16)


def scales_of(ref, count):
    powers = jnp.exp2(ref[WEEK:CODED, :].astype(jnp.int32).astype(F32)) * (1.0 / TOP)
    return [powers[b:b + 1, :] for b in range(count)]


def decode(ref, count):
    scales = scales_of(ref, count)
    return [ref[b * BAND:(b + 1) * BAND, :].astype(jnp.int32).astype(F32) * scales[b] for b in range(count)]


def greet(peers):
    barrier = pltpu.get_barrier_semaphore()
    for peer in peers:
        pl.semaphore_signal(barrier, inc=1, device_id=peer, device_id_type=MESH)
    pl.semaphore_wait(barrier, len(peers))


def obs_peers(o):
    z, c = o // 2, o % 2

    def at(step, core):
        return ((z + step + CHIPS) % CHIPS) * 2 + core

    return z, c, at


def remote(src, dst, sems, at, to):
    send, recv = sems
    return pltpu.make_async_remote_copy(
        src_ref=src, dst_ref=dst, send_sem=send.at[at], recv_sem=recv.at[at], device_id=to, device_id_type=MESH,
    )


class Gather:
    def __init__(self, own_ref, out_ref, o, sems, local):
        self.own, self.out, self.o, self.sems = own_ref, out_ref, o, sems
        self.z, self.c, self.at = obs_peers(o)
        self.partner, self.up, self.down = ({"obs": self.at(*p)} for p in ((0, 1 - self.c), (1, self.c), (-1, self.c)))
        self.weeks = own_ref.shape[0]
        self.keep = [pltpu.make_async_copy(own_ref.at[w], out_ref.at[o, w], local.at[w]) for w in range(self.weeks)]
        self.started = []

    def copy(self, role, w, step, core, to):
        ref = self.out.at[self.at(step, core), w]
        return remote(self.own.at[w] if role < 3 else ref, self.out.at[self.o, w] if role < 3 else ref, self.sems, (role, w), to)

    def arrival(self, role, w, step, core):
        ref = self.out.at[self.at(step, core), w]
        remote(self.own.at[w], ref, self.sems, (role, w), self.partner).wait_recv()

    def start(self, *copies):
        for one in copies:
            one.start()
        self.started += copies

    def far_way(self, w):
        return (3, -1, self.up) if w < 2 else (3, 1, self.down)

    def send(self, w):
        self.start(self.copy(1, w, 0, self.c, self.up), self.copy(2, w, 0, self.c, self.down), self.copy(0, w, 0, self.c, self.partner))
        self.keep[w].start()

    def forward(self, w):
        for role, step in ((1, -1), (2, 1)) if w < 2 else ((2, 1), (1, -1)):
            self.arrival(role, w, step, self.c)
            far, far_step, way = self.far_way(w)
            if step == far_step:
                self.start(self.copy(far, w, step, self.c, way))
            self.start(self.copy(3 + role, w, step, self.c, self.partner))

    def relay(self, w):
        self.arrival(3, w, 2, self.c)
        self.start(self.copy(6, w, 2, self.c, self.partner))

    def complete(self, w):
        for role, step in ((0, 0), (4, -1), (5, 1), (6, 2)):
            self.arrival(role, w, step, 1 - self.c)
        self.keep[w].wait()

    def finish(self):
        for one in self.started:
            one.wait_send()


def run_gather(gather, order, produce, consume):
    for n, w in enumerate(order):
        produce(w)
        gather.send(w)
        if n >= 1:
            gather.forward(order[n - 1])
        if n >= 2:
            gather.relay(order[n - 2])
        if n >= 3:
            gather.complete(order[n - 3])
            consume(order[n - 3])
    gather.forward(order[-1])
    gather.relay(order[-2])
    gather.complete(order[-3])
    consume(order[-3])
    gather.relay(order[-1])
    for w in order[-2:]:
        gather.complete(w)
        consume(w)
    gather.finish()


def halo_copies(src_ref, halo_ref, w, l, bands, sems):
    return [
        remote(src_ref.at[w], halo_ref.at[slot, w], sems, (slot, w), {"lat": (l + step) % bands})
        for slot, step in ((0, 1), (1, bands - 1))
    ]


def stacks_of(low, mid, high):
    return [jnp.concatenate(three, axis=0) for three in zip(low, mid, high)]


def blocks_of(ref, count):
    return [ref[b * BAND:(b + 1) * BAND, :] for b in range(count)]


def put_blocks(ref, blocks):
    for b, value in enumerate(blocks):
        ref[b * BAND:(b + 1) * BAND, :] = value.astype(ref.dtype)


def spread_kernel(sizes, direction_ref, widths_ref, out_ref, field, smooth, wire, halo, shard, send, recv, hsend, hrecv, load, local):
    o, l = lax.axis_index("obs"), lax.axis_index("lat")
    bands, weeks, count, bits, lat_decay, lon_decay = sizes
    loads = [pltpu.make_async_copy(direction_ref.at[o, w], field.at[w], load.at[w]) for w in range(weeks)]
    for one in loads:
        one.start()
    z, c, at = obs_peers(o)
    greet([{"obs": at(0, 1 - c)}, {"obs": at(1, c)}, {"obs": at(-1, c)},
           {"lat": (l + 1) % bands}, {"lat": (l + bands - 1) % bands}])
    lon_width = down_rows(widths_ref[0:1, :])[0:BAND]
    weights = lat_rows(widths_ref, lat_decay, l, bands, False)
    halos = []

    def begin(w):
        loads[w].wait()
        done = along_lon([field[w, :, b * EDGE:(b + 1) * EDGE] for b in range(count)], lon_width, lon_decay, bits)
        encode(wire.at[w], done)
        halos.append(halo_copies(wire, halo, w, l, bands, (hsend, hrecv)))
        for one in halos[w]:
            one.start()
        put_blocks(smooth.at[w], done)

    begin(0)
    begin(1)

    def produce(w):
        if w + 2 < weeks:
            begin(w + 2)
        for one in halos[w]:
            one.wait_recv()
        stacks = stacks_of(decode(halo.at[0, w], count), blocks_of(smooth.at[w], count), decode(halo.at[1, w], count))
        put_blocks(shard.at[w], mix_rows(weights, stacks))

    run_gather(Gather(shard, out_ref, o, (send, recv), local), range(weeks), produce, lambda w: None)
    for pair_of in halos:
        for one in pair_of:
            one.wait_send()


def pair(first, second):
    none = jnp.zeros_like(first)
    return jnp.concatenate([jnp.concatenate([first, none], axis=1), jnp.concatenate([none, second], axis=1)], axis=0)


def place_of(col):
    row = (col * 6554) >> 15
    return pl.ds((row >> 5) * WEEK + (col - 5 * row) * BAND + (row & 31), 8, stride=STEP)


def factor_of(scale):
    return (8 >> scale).astype(F32) * 0.125


def forward_kernel(per_step, rows_ref, cols_ref, scale_ref, cells_ref, blocks_ref, out_ref, cells):
    step = pl.program_id(0)

    @pl.when(step == 0)
    def _():
        for k in range(8):
            cells[k * STEP:k * STEP + FIELD, :] = cells_ref[k * FIELD:(k + 1) * FIELD, :].astype(F32)
        out_ref[...] = jnp.zeros_like(out_ref)

    def two(n, carry):
        at = [step * per_step + 2 * n + i for i in range(2)]
        picked = pair(*[cells[place_of(cols_ref[0, 0, a]), :].astype(BF16) for a in at])
        both = jnp.concatenate([blocks_ref[2 * n], blocks_ref[2 * n + 1]], axis=1)
        value = lax.dot_general(picked, both, (((1,), (1,)), ((), ())), preferred_element_type=F32)
        for i, a in enumerate(at):
            row = rows_ref[0, 0, a]
            out_ref[row] = out_ref[row] + value[8 * i:8 * i + 8] * factor_of(scale_ref[0, 0, a])
        return carry

    lax.fori_loop(0, per_step // 2, two, 0, unroll=8)


def adjoint_kernel(per_step, rows_ref, cols_ref, scale_ref, values_ref, blocks_ref, out_ref, total):
    step = pl.program_id(0)

    @pl.when(step == 0)
    def _():
        total[...] = jnp.zeros_like(total)

    def two(n, carry):
        at = [step * per_step + 2 * n + i for i in range(2)]
        pulled = jnp.concatenate([values_ref[rows_ref[0, 0, a]] for a in at], axis=0)
        both = jnp.concatenate([blocks_ref[2 * n], blocks_ref[2 * n + 1]], axis=1)
        value = jnp.dot(pulled, both, preferred_element_type=F32)
        for i, a in enumerate(at):
            place = place_of(cols_ref[0, 0, a])
            part = value[8 * i:8 * i + 8, EDGE * i:EDGE * i + EDGE]
            total[place, :] = total[place, :] + part * factor_of(scale_ref[0, 0, a])
        return carry

    lax.fori_loop(0, per_step // 2, two, 0, unroll=8)

    @pl.when(step == pl.num_programs(0) - 1)
    def _():
        for k in range(8):
            out_ref[k * FIELD:(k + 1) * FIELD, :] = total[k * STEP:k * STEP + FIELD, :]


def sum_bands_kernel(bands, part_ref, weight_ref, out_ref, got, shard, send, recv, send2, recv2):
    l = lax.axis_index("lat")
    share = part_ref.shape[0] // bands
    greet([{"lat": (l + d) % bands} for d in range(1, bands)])
    mine = pl.ds(l * share, share)

    def first(d):
        peer = (l + d) % bands
        return pltpu.make_async_remote_copy(
            src_ref=part_ref.at[pl.ds(peer * share, share)], dst_ref=got.at[d], send_sem=send.at[d], recv_sem=recv.at[d],
            device_id={"lat": peer}, device_id_type=MESH,
        )

    def second(d, owner):
        return pltpu.make_async_remote_copy(
            src_ref=shard, dst_ref=out_ref.at[pl.ds(owner * share, share)], send_sem=send2.at[d], recv_sem=recv2.at[d],
            device_id={"lat": (l + d) % bands}, device_id_type=MESH,
        )

    for d in range(1, bands):
        first(d).start()
    total = part_ref[mine]
    for d in range(1, bands):
        first(d).wait_recv()
        total = total + got[d]
    weight = weight_ref[mine]
    shard[...] = (total * weight).astype(shard.dtype)
    for d in range(1, bands):
        second(d, l).start()
    out_ref[mine] = shard[...]
    for d in range(1, bands):
        second(d, (l + bands - d) % bands).wait_recv()
    for d in range(1, bands):
        first(d).wait_send()
        second(d, l).wait_send()


def image_kernel(sizes, part_ref, widths_ref, residual_ref, direction_ref, out_ref, coef_ref, own, there, far_out, near_out,
                 relay_out, far_in, near_in, relay_in, mine, band, halo, shard, everyone, res, dire, sums, line_got, line_sum,
                 send, recv, hsend, hrecv, psend, precv, rsend, rrecv, lsend, lrecv, load, local, fields, leave):
    o, l = lax.axis_index("obs"), lax.axis_index("lat")
    bands, weeks, count, bits, lat_decay, lon_decay = sizes
    z, c, at = obs_peers(o)
    partner, up, down = {"obs": at(0, 1 - c)}, {"obs": at(1, c)}, {"obs": at(-1, c)}
    k, side = 2 * CHIPS, CHIPS
    x, y = l // side, l % side
    lines = [[{"lat": x * side + (y + d) % side} for d in range(1, side)], [{"lat": (x + d) % side * side + y} for d in range(1, side)]]
    gets = [pltpu.make_async_copy(residual_ref, res, fields.at[0]), pltpu.make_async_copy(direction_ref, dire, fields.at[1])]
    greet([partner, up, down, {"lat": (l + 1) % bands}, {"lat": (l + bands - 1) % bands}, *lines[0], *lines[1]])
    order = (0, 2, 1, 3)

    def rows_for(core, w):
        return part_ref.at[:, core, w]

    swaps = [remote(rows_for(1 - c, w), there.at[w], (psend, precv), w, partner) for w in range(weeks)]
    loads = [pltpu.make_async_copy(rows_for(c, w), own.at[w], load.at[w]) for w in range(weeks)]
    for w in order:
        swaps[w].start()
        loads[w].start()
    for one in gets:
        one.start()
    sums[...] = jnp.zeros_like(sums)
    lon_width = down_rows(widths_ref[0:1, :])[0:BAND]
    weights = lat_rows(widths_ref, lat_decay, l, bands, True)
    ring = (rsend, rrecv)

    def way(w):
        return (1, up, down) if w < 2 else (-1, down, up)

    far = [remote(far_out.at[w], far_in.at[w], ring, (0, w), way(w)[1]) for w in range(weeks)]
    relayed = [remote(relay_out.at[w], relay_in.at[w], ring, (1, w), way(w)[1]) for w in range(weeks)]
    near = [remote(near_out.at[w], near_in.at[w], ring, (2, w), way(w)[2]) for w in range(weeks)]
    halos = [halo_copies(band, halo, w, l, bands, (hsend, hrecv)) for w in range(weeks)]

    def chip_sum(w, step):
        there_too = (z + step + CHIPS) % CHIPS
        return [x + y for x, y in zip(blocks_of(own.at[w, there_too], count), blocks_of(there.at[w, there_too], count))]

    def plus(x, y):
        return [a + d for a, d in zip(x, y)]

    for w in order:
        swaps[w].wait_recv()
        loads[w].wait()
        encode(far_out.at[w], chip_sum(w, 2))
        far[w].start()
        encode(near_out.at[w], chip_sum(w, -way(w)[0]))
        near[w].start()
    gets[0].wait()
    for w in (0, 1):
        gram_first(k, count, w, res, sums)
    for w in order:
        far[w].wait_recv()
        encode(relay_out.at[w], plus(chip_sum(w, way(w)[0]), decode(far_in.at[w], count)))
        relayed[w].start()
    for w in order:
        if w == order[0]:
            for early in (2, 3):
                gram_first(k, count, early, res, sums)
            gets[1].wait()
        near[w].wait_recv()
        relayed[w].wait_recv()
        total = plus(plus(chip_sum(w, 0), decode(near_in.at[w], count)), decode(relay_in.at[w], count))
        encode(band.at[w], total)
        for one in halos[w]:
            one.start()
        put_blocks(mine.at[w], total)

    def produce(w):
        for one in halos[w]:
            one.wait_recv()
        stacks = stacks_of(decode(halo.at[0, w], count), blocks_of(mine.at[w], count), decode(halo.at[1, w], count))
        encode(shard.at[w], along_lon(mix_rows(weights, stacks), lon_width, lon_decay, bits))

    leaving = [pltpu.make_async_copy(everyone.at[:, w], out_ref.at[:, w], leave.at[w]) for w in range(weeks)]

    def consume(w):
        leaving[w].start()
        gram_week(k, count, w, res, dire, everyone, sums)

    run_gather(Gather(shard, everyone, o, (send, recv), local), order, produce, consume)
    total = gram_total(k, sums)
    for axis, here in ((0, y), (1, x)):
        line_sum[axis] = total
        copies = [remote(line_sum.at[axis], line_got.at[axis, here], (lsend, lrecv), (axis, d), to) for d, to in enumerate(lines[axis])]
        for one in copies:
            one.start()
        line_got[axis, here] = total
        for d in range(side - 1):
            back = (here + side - 1 - d) % side
            remote(line_sum.at[axis], line_got.at[axis, back], (lsend, lrecv), (axis, d), lines[axis][d]).wait_recv()
        total = line_got[axis, 0] + line_got[axis, 1] + line_got[axis, 2] + line_got[axis, 3]
        for one in copies:
            one.wait_send()
    coef_ref[...] = coefficients(total)
    for w in range(weeks):
        leaving[w].wait()
        for one in (swaps[w], far[w], relayed[w], near[w], *halos[w]):
            one.wait_send()


def change_block(change_ref, i, w, b, first, rows):
    at = b * BAND + first
    at = at if isinstance(at, int) else pl.multiple_of(at, 16)
    power = change_ref[i, w, WEEK:CODED, :].astype(jnp.int32).astype(F32)
    pick = jnp.sum(jnp.where(iota((16, EDGE), 0) == b, power, 0.0), axis=0, keepdims=True)
    return change_ref[i, w, pl.ds(at, rows), :].astype(jnp.int32).astype(F32) * (jnp.exp2(pick) * (1.0 / TOP))


def add_gram(sums, t, i, j, x, y):
    sums[t, i, j] = sums[t, i, j] + jnp.sum((x * y).reshape(BAND // 8, 8, EDGE), axis=0)


def lanes_of(b):
    return pl.ds(pl.multiple_of(b * EDGE, EDGE), EDGE)


def gram_first(k, count, w, res_ref, sums):
    def one(b, carry):
        res = [res_ref[i, w, :, lanes_of(b)] for i in range(k)]
        for i in range(k):
            for j in range(i, k):
                add_gram(sums, 0, i, j, res[i], res[j])
        return carry

    lax.fori_loop(0, count, one, 0)


def gram_week(k, count, w, res_ref, dire_ref, change_ref, sums):
    def one(b, carry):
        res = [res_ref[i, w, :, lanes_of(b)] for i in range(k)]
        dire = [dire_ref[i, w, :, lanes_of(b)] for i in range(k)]
        img = [dire[i] + change_block(change_ref, i, w, b, 0, BAND) for i in range(k)]
        for i in range(k):
            for j in range(k):
                if i <= j:
                    add_gram(sums, 3, i, j, img[i], img[j])
                add_gram(sums, 1, i, j, dire[i], img[j])
                add_gram(sums, 2, i, j, img[i], res[j])
        return carry

    lax.fori_loop(0, count, one, 0)


def gram_total(k, sums):
    lane = iota((k, EDGE), 1)
    result = jnp.zeros((k, EDGE), F32)
    for t in range(4):
        for i in range(k):
            line = jnp.sum(jnp.sum(sums[t, i], axis=1), axis=1, keepdims=True)
            result = jnp.where(lane == t * k + i, jnp.broadcast_to(line, (k, EDGE)), result)
    return result


def flip(x):
    square = jnp.concatenate([x, jnp.zeros((EDGE - 8, EDGE), F32)], axis=0)
    return jnp.transpose(square)[:8, :]


def product(x, y):
    return sum(jnp.broadcast_to(x[:, i:i + 1], (8, EDGE)) * jnp.broadcast_to(y[i:i + 1, :], (8, EDGE)) for i in range(8))


def solve(a, b):
    row = iota((8, EDGE), 0)
    for p in range(8):
        line = jnp.broadcast_to(a[p:p + 1, :], (8, EDGE))
        line_b = jnp.broadcast_to(b[p:p + 1, :], (8, EDGE))
        column = jnp.broadcast_to(a[:, p:p + 1], (8, EDGE))
        inverse = 1.0 / jnp.broadcast_to(a[p:p + 1, p:p + 1], (8, EDGE))
        ratio = column * inverse
        here = row == p
        a = jnp.where(here, line * inverse, a - ratio * line)
        b = jnp.where(here, line_b * inverse, b - ratio * line_b)
    return b


def coefficients(total):
    lane, row = iota((8, EDGE), 1), iota((8, EDGE), 0)
    parts = []
    for t in range(4):
        moved = total if t == 0 else pltpu.roll(total, EDGE - 8 * t, 1)
        parts.append(jnp.where(lane < 8, moved, 0.0))

    def full(x):
        low = jnp.where(lane <= row, x, 0.0)
        return low + flip(jnp.where(lane < row, x, 0.0))

    gram_old, image_image = full(parts[0]), full(parts[3])
    curvature = 0.5 * (parts[1] + flip(parts[1]))
    residual_image = parts[2]
    step = solve(curvature, gram_old)
    cross = product(residual_image, step)
    gram_new = gram_old - cross - flip(cross) + product(flip(step), product(image_image, step))
    turn = solve(gram_old, gram_new)
    return jnp.where(lane < 8, step, 0.0) + pltpu.roll(jnp.where(lane < 8, turn, 0.0), 8, 1)


def update_kernel(k, coef_ref, solution_ref, residual_ref, direction_ref, change_ref, sol_out, res_out, dir_out):
    rows_each = 32

    def one(b, carry):
        lanes = pl.ds(pl.multiple_of(b * EDGE, EDGE), EDGE)
        for r in range(BAND // rows_each):
            rows = slice(r * rows_each, (r + 1) * rows_each)
            dire = [direction_ref[i, 0, rows, lanes] for i in range(k)]
            more = [change_block(change_ref, i, 0, b, r * rows_each, rows_each) for i in range(k)]
            for a in range(k):
                forth = sum(coef_ref[i, a] * dire[i] for i in range(k))
                back = sum(coef_ref[i, a] * more[i] for i in range(k))
                turn = sum(coef_ref[i, k + a] * dire[i] for i in range(k))
                left = residual_ref[a, 0, rows, lanes] - (forth + back)
                sol_out[a, 0, rows, lanes] = solution_ref[a, 0, rows, lanes] + forth
                res_out[a, 0, rows, lanes] = left
                dir_out[a, 0, rows, lanes] = left + turn
        return carry

    lax.fori_loop(0, 5, one, 0)


def params(collective=None, limit=None):
    extra = {} if collective is None else {"collective_id": collective, "has_side_effects": True}
    return pltpu.CompilerParams(vmem_limit_bytes=limit or (48 << 20), **extra)


def shards(bands, footprints, block_rows, block_cols, block_scale, lat_width, lon_width, obs_weight, solution, residual, direction):
    k, weeks, band_rows, nlon = direction.shape
    blocks = footprints.shape[2]
    count = nlon // EDGE
    assert (k, weeks, band_rows, count, bands) == (8, 4, BAND, 5, CHIPS * CHIPS)
    row_blocks = obs_weight.shape[0] // EDGE
    sizes = (bands, weeks, count, (nlon // 8 + 1).bit_length(), band_rows / 2.0, nlon / 32.0)
    l = lax.axis_index("lat")
    lon_own = lax.dynamic_slice_in_dim(lon_width, l * BAND, BAND)
    lat_near = lax.dynamic_slice_in_dim(jnp.pad(lat_width, BAND), l * BAND, 3 * BAND)
    widths = jnp.pad(jnp.stack([jnp.pad(lon_own, (0, 3 * BAND)), jnp.pad(lat_near, (0, BAND))]), ((0, 6), (0, 0))).astype(F32)
    all_rows = k * weeks * WEEK
    plain, coded = (weeks, WEEK, EDGE), (weeks, CODED, EDGE)
    ints = jnp.int16

    cells = pl.pallas_call(
        functools.partial(spread_kernel, sizes),
        out_shape=jax.ShapeDtypeStruct((k, *plain), BF16),
        in_specs=[ANY_SPEC, VMEM_SPEC],
        out_specs=ANY_SPEC,
        scratch_shapes=[
            VMEM((weeks, band_rows, nlon), F32), VMEM(plain, F32), VMEM(coded, ints), VMEM((2, *coded), ints), VMEM(plain, BF16),
            DMA((7, weeks)), DMA((7, weeks)), DMA((2, weeks)), DMA((2, weeks)), DMA((weeks,)), DMA((weeks,)),
        ],
        compiler_params=params(1, 64_450_000),
        name="spread",
    )(direction, widths)

    per_step = 48
    smem = [SMEM_SPEC] * 3
    block_spec = pl.BlockSpec((None, None, per_step, EDGE, EDGE), lambda i: (0, 0, i, 0, 0))
    forward = pl.pallas_call(
        functools.partial(forward_kernel, per_step),
        grid=(blocks // per_step,),
        out_shape=jax.ShapeDtypeStruct((row_blocks, k, EDGE), F32),
        in_specs=smem + [pl.BlockSpec((all_rows, EDGE), lambda i: (0, 0)), block_spec],
        out_specs=pl.BlockSpec((row_blocks, k, EDGE), lambda i: (0, 0, 0)),
        scratch_shapes=[VMEM((k * STEP, EDGE), F32)],
        compiler_params=params(),
        name="forward",
    )(block_rows, block_cols, block_scale, cells.reshape(all_rows, EDGE), footprints)

    share = row_blocks // bands
    values = pl.pallas_call(
        functools.partial(sum_bands_kernel, bands),
        out_shape=jax.ShapeDtypeStruct((row_blocks, k, EDGE), BF16),
        in_specs=[VMEM_SPEC, VMEM_SPEC],
        out_specs=VMEM_SPEC,
        scratch_shapes=[
            VMEM((bands, share, k, EDGE), F32), VMEM((share, k, EDGE), BF16),
            DMA((bands,)), DMA((bands,)), DMA((bands,)), DMA((bands,)),
        ],
        compiler_params=params(2),
        name="sum_bands",
    )(forward, obs_weight.reshape(row_blocks, 1, EDGE))

    part = pl.pallas_call(
        functools.partial(adjoint_kernel, per_step),
        grid=(blocks // per_step,),
        out_shape=jax.ShapeDtypeStruct((all_rows, EDGE), F32),
        in_specs=smem + [pl.BlockSpec((row_blocks, k, EDGE), lambda i: (0, 0, 0)), block_spec],
        out_specs=pl.BlockSpec((all_rows, EDGE), lambda i: (0, 0)),
        scratch_shapes=[VMEM((k * STEP, EDGE), F32)],
        compiler_params=params(),
        name="adjoint",
    )(block_rows, block_cols, block_scale, values, footprints)

    side = CHIPS
    change, coef = pl.pallas_call(
        functools.partial(image_kernel, sizes),
        out_shape=[jax.ShapeDtypeStruct((k, *coded), ints), jax.ShapeDtypeStruct((k, EDGE), F32)],
        in_specs=[ANY_SPEC, VMEM_SPEC, ANY_SPEC, ANY_SPEC],
        out_specs=[ANY_SPEC, VMEM_SPEC],
        scratch_shapes=[
            VMEM((weeks, CHIPS, WEEK, EDGE), F32), VMEM((weeks, CHIPS, WEEK, EDGE), F32),
            *[VMEM(coded, ints)] * 6, VMEM(plain, F32), VMEM(coded, ints), VMEM((2, *coded), ints), VMEM(coded, ints),
            VMEM((k, *coded), ints), VMEM(direction.shape, F32), VMEM(direction.shape, F32), VMEM((4, k, k, 8, EDGE), F32),
            VMEM((2, side, k, EDGE), F32), VMEM((2, k, EDGE), F32),
            DMA((7, weeks)), DMA((7, weeks)), DMA((2, weeks)), DMA((2, weeks)), DMA((weeks,)), DMA((weeks,)),
            DMA((3, weeks)), DMA((3, weeks)), DMA((2, side - 1)), DMA((2, side - 1)), DMA((weeks,)), DMA((weeks,)),
            DMA((2,)), DMA((weeks,)),
        ],
        compiler_params=params(3),
        name="image",
    )(part.reshape(CHIPS, 2, *plain), widths, residual, direction)

    native = pl.BlockSpec((k, 1, band_rows, nlon), lambda w: (0, w, 0, 0))
    packed = pl.BlockSpec((k, 1, CODED, EDGE), lambda w: (0, w, 0, 0))
    return pl.pallas_call(
        functools.partial(update_kernel, k),
        grid=(weeks,),
        out_shape=[jax.ShapeDtypeStruct(direction.shape, F32)] * 3,
        in_specs=[SMEM_SPEC, native, native, native, packed],
        out_specs=[native] * 3,
        compiler_params=params(),
        name="update",
    )(coef, solution, residual, direction, change)


def solution(mesh):
    assert mesh.shape["obs"] == 2 * CHIPS
    three = (P(None, None, "lat", None),) * 3
    blocks = P("obs", "lat", None)
    return jax.shard_map(
        functools.partial(shards, mesh.shape["lat"]),
        mesh=mesh,
        in_specs=(P("obs", "lat", None, None, None), blocks, blocks, blocks, P(), P(), P("obs"), *three),
        out_specs=three,
        check_vma=False,
    )
```

```python
import functools

import jax
import jax.numpy as jnp
from jax import lax
from jax.experimental import pallas as pl
from jax.experimental.pallas import tpu as pltpu
from jax.sharding import PartitionSpec as P

MESH = pl.DeviceIdType.MESH
HIGHEST = lax.Precision.HIGHEST
F32 = jnp.float32
BF16 = jnp.bfloat16
VMEM = pltpu.VMEM
DMA = pltpu.SemaphoreType.DMA
EDGE = 128
CHIPS = 4
ANY_SPEC = pl.BlockSpec(memory_space=pl.ANY)
VMEM_SPEC = pl.BlockSpec(memory_space=pltpu.VMEM)
SMEM_SPEC = pl.BlockSpec(memory_space=pltpu.SMEM)
BAND = 32
WEEK = 160
CODED = WEEK + 16
FIELD = 640
STEP = FIELD + 1
TOP = 32000.0


def iota(shape, axis):
    return lax.broadcasted_iota(jnp.int32, shape, axis)


def norm_of(width, decay):
    p = jnp.exp(jnp.full_like(width, -2.0 / decay))
    return jnp.sqrt(1.0 + 2.0 * p * (1.0 - jnp.exp(width * (-2.0 / decay))) / (1.0 - p))


def down_rows(ref, first):
    row = iota((BAND, EDGE), 0)
    result = jnp.zeros((BAND, EDGE), jnp.int32)
    for r in range(BAND):
        result = jnp.where(row == r, ref[first + r], result)
    return result.astype(F32)


def along_lanes(ref, first, count):
    lane = iota((1, EDGE), 1)
    result = jnp.zeros((1, EDGE), jnp.int32)
    for c in range(count):
        result = jnp.where(lane == c, ref[(first + c) % ref.shape[0]], result)
    return result.astype(F32)


def along_lon(blocks, width, decay, bits):
    rows = blocks[0].shape[0]
    count = len(blocks)
    lane = iota((rows, EDGE), 1)
    terms = width.astype(jnp.int32) + 1
    picks = [((terms >> m) & 1) == 1 for m in range(bits)]

    def shifted(values, step, sign):
        turned = [pltpu.roll(v, step if sign > 0 else EDGE - step, 1) for v in values]
        inside = lane >= step if sign > 0 else lane < EDGE - step
        return [jnp.where(inside, turned[b], turned[(b - sign) % count]) for b in range(count)]

    sides = []
    for sign in (1, -1):
        power = blocks
        total = [jnp.where(picks[0], v, 0.0) for v in blocks]
        for m in range(1, bits):
            half = 2 ** (m - 1)
            moved = shifted(power, half, sign)
            fade = jnp.exp(jnp.full((rows, EDGE), -half / decay, F32))
            power = [a + fade * c for a, c in zip(power, moved)]
            moved = shifted(total, 2 * half, sign)
            fade = fade * fade
            total = [jnp.where(picks[m], a + fade * c, t) for a, c, t in zip(power, moved, total)]
        sides.append(total)
    scale = 1.0 / norm_of(width, decay)
    return [(up + down - x) * scale for up, down, x in zip(sides[0], sides[1], blocks)]


def lat_rows(widths, reach, l, bands, across):
    r, c = iota((BAND, EDGE), 0), iota((BAND, EDGE), 1)
    width = along_lanes(widths, (l + bands - 1) * BAND, 3 * BAND) if across else down_rows(widths, l * BAND)
    distance = jnp.abs(r - c + BAND).astype(F32)
    low = jnp.where(l > 0, 0, BAND)
    high = jnp.where(l < bands - 1, 3 * BAND, 2 * BAND)
    value = jnp.exp(-distance / reach) / norm_of(width, reach)
    return jnp.where((distance <= width) & (c >= low) & (c < high), value, 0.0)


def mix_rows(weights, stacks):
    weights = weights[:, :3 * BAND]
    large = weights.astype(BF16)
    both = jnp.concatenate([large, (weights - large.astype(F32)).astype(BF16)], axis=0)
    stack = jnp.concatenate(stacks, axis=1)
    first = stack.astype(BF16)
    second = (stack - first.astype(F32)).astype(BF16)
    main = jnp.dot(both, first, preferred_element_type=F32)
    total = main[:BAND] + (main[BAND:] + jnp.dot(large, second, preferred_element_type=F32))
    return [total[:, b * EDGE:(b + 1) * EDGE] for b in range(len(stacks))]


def encode(ref, blocks):
    row = iota((16, EDGE), 0)
    powers = jnp.zeros((16, EDGE), F32)
    for b, value in enumerate(blocks):
        top = jnp.max(jnp.abs(value), axis=0, keepdims=True)
        power = jnp.ceil(jnp.log2(jnp.maximum(top, 1e-30)))
        whole = jnp.round(value * (jnp.exp2(-power) * TOP))
        ref[b * BAND:(b + 1) * BAND, :] = whole.astype(jnp.int32).astype(jnp.int16)
        powers = jnp.where(row == b, jnp.broadcast_to(power, (16, EDGE)), powers)
    ref[WEEK:CODED, :] = powers.astype(jnp.int32).astype(jnp.int16)


def scales_of(ref, count):
    powers = jnp.exp2(ref[WEEK:CODED, :].astype(jnp.int32).astype(F32)) * (1.0 / TOP)
    return [powers[b:b + 1, :] for b in range(count)]


def decode(ref, count):
    scales = scales_of(ref, count)
    return [ref[b * BAND:(b + 1) * BAND, :].astype(jnp.int32).astype(F32) * scales[b] for b in range(count)]


def greet(peers):
    barrier = pltpu.get_barrier_semaphore()
    for peer in peers:
        pl.semaphore_signal(barrier, inc=1, device_id=peer, device_id_type=MESH)
    pl.semaphore_wait(barrier, len(peers))


def obs_peers(o):
    z, c = o // 2, o % 2

    def at(step, core):
        return ((z + step + CHIPS) % CHIPS) * 2 + core

    return z, c, at


def remote(src, dst, sems, at, to):
    send, recv = sems
    return pltpu.make_async_remote_copy(
        src_ref=src, dst_ref=dst, send_sem=send.at[at], recv_sem=recv.at[at], device_id=to, device_id_type=MESH,
    )


class Gather:
    def __init__(self, own_ref, out_ref, o, sems, local):
        self.own, self.out, self.o, self.sems = own_ref, out_ref, o, sems
        self.z, self.c, self.at = obs_peers(o)
        self.partner, self.up, self.down = ({"obs": self.at(*p)} for p in ((0, 1 - self.c), (1, self.c), (-1, self.c)))
        self.weeks = own_ref.shape[0]
        self.keep = [pltpu.make_async_copy(own_ref.at[w], out_ref.at[o, w], local.at[w]) for w in range(self.weeks)]
        self.started = []

    def copy(self, role, w, step, core, to):
        ref = self.out.at[self.at(step, core), w]
        return remote(self.own.at[w] if role < 3 else ref, self.out.at[self.o, w] if role < 3 else ref, self.sems, (role, w), to)

    def arrival(self, role, w, step, core):
        ref = self.out.at[self.at(step, core), w]
        remote(self.own.at[w], ref, self.sems, (role, w), self.partner).wait_recv()

    def start(self, *copies):
        for one in copies:
            one.start()
        self.started += copies

    def far_way(self, w):
        return (3, -1, self.up) if w < 2 else (3, 1, self.down)

    def send(self, w):
        self.start(self.copy(1, w, 0, self.c, self.up), self.copy(2, w, 0, self.c, self.down), self.copy(0, w, 0, self.c, self.partner))
        self.keep[w].start()

    def forward(self, w):
        for role, step in ((1, -1), (2, 1)) if w < 2 else ((2, 1), (1, -1)):
            self.arrival(role, w, step, self.c)
            far, far_step, way = self.far_way(w)
            if step == far_step:
                self.start(self.copy(far, w, step, self.c, way))
            self.start(self.copy(3 + role, w, step, self.c, self.partner))

    def relay(self, w):
        self.arrival(3, w, 2, self.c)
        self.start(self.copy(6, w, 2, self.c, self.partner))

    def complete(self, w):
        for role, step in ((0, 0), (4, -1), (5, 1), (6, 2)):
            self.arrival(role, w, step, 1 - self.c)
        self.keep[w].wait()

    def finish(self):
        for one in self.started:
            one.wait_send()


def run_gather(gather, order, produce, consume):
    def finish_week(w):
        gather.complete(w)
        consume(w)

    a, b, c, d = order
    for w, late in ((a, None), (b, None), (c, a), (d, b)):
        produce(w)
        gather.send(w)
        if late is not None:
            gather.forward(late)
    gather.forward(c)
    gather.relay(a)
    gather.forward(d)
    gather.relay(b)
    finish_week(a)
    gather.relay(c)
    gather.relay(d)
    for w in (b, c, d):
        finish_week(w)
    gather.finish()


def halo_copies(src_ref, halo_ref, w, l, bands, sems):
    return [
        remote(src_ref.at[w], halo_ref.at[slot, w], sems, (slot, w), {"lat": (l + step) % bands})
        for slot, step in ((0, 1), (1, bands - 1))
    ]


def stacks_of(low, mid, high):
    return [jnp.concatenate(three, axis=0) for three in zip(low, mid, high)]


def blocks_of(ref, count):
    return [ref[b * BAND:(b + 1) * BAND, :] for b in range(count)]


def put_blocks(ref, blocks):
    for b, value in enumerate(blocks):
        ref[b * BAND:(b + 1) * BAND, :] = value.astype(ref.dtype)


def spread_kernel(sizes, direction_ref, lat_ref, lon_ref, out_ref, field, smooth, wire, halo, shard, send, recv, hsend, hrecv, load, local):
    o, l = lax.axis_index("obs"), lax.axis_index("lat")
    bands, weeks, count, bits, lat_decay, lon_decay = sizes
    loads = [pltpu.make_async_copy(direction_ref.at[o, w], field.at[w], load.at[w]) for w in range(weeks)]
    for one in loads:
        one.start()
    z, c, at = obs_peers(o)
    greet([{"obs": at(0, 1 - c)}, {"obs": at(1, c)}, {"obs": at(-1, c)},
           {"lat": (l + 1) % bands}, {"lat": (l + bands - 1) % bands}])
    lon_width = down_rows(lon_ref, l * BAND)
    weights = lat_rows(lat_ref, lat_decay, l, bands, False)
    halos = []

    def begin(w):
        loads[w].wait()
        done = along_lon([field[w, :, b * EDGE:(b + 1) * EDGE] for b in range(count)], lon_width, lon_decay, bits)
        encode(wire.at[w], done)
        halos.append(halo_copies(wire, halo, w, l, bands, (hsend, hrecv)))
        for one in halos[w]:
            one.start()
        put_blocks(smooth.at[w], done)

    begin(0)
    begin(1)

    def produce(w):
        if w + 2 < weeks:
            begin(w + 2)
        for one in halos[w]:
            one.wait_recv()
        stacks = stacks_of(decode(halo.at[0, w], count), blocks_of(smooth.at[w], count), decode(halo.at[1, w], count))
        put_blocks(shard.at[w], mix_rows(weights, stacks))

    run_gather(Gather(shard, out_ref, o, (send, recv), local), range(weeks), produce, lambda w: None)
    for pair_of in halos:
        for one in pair_of:
            one.wait_send()


def pair(first, second):
    none = jnp.zeros_like(first)
    return jnp.concatenate([jnp.concatenate([first, none], axis=1), jnp.concatenate([none, second], axis=1)], axis=0)


def place_of(col):
    row = (col * 6554) >> 15
    return pl.ds((row >> 5) * WEEK + (col - 5 * row) * BAND + (row & 31), 8, stride=STEP)


def factor_of(scale):
    return (8 >> scale).astype(F32) * 0.125


def forward_kernel(per_step, rows_ref, cols_ref, scale_ref, cells_ref, blocks_ref, out_ref, cells):
    step = pl.program_id(0)

    @pl.when(step == 0)
    def _():
        for k in range(8):
            cells[k * STEP:k * STEP + FIELD, :] = cells_ref[k * FIELD:(k + 1) * FIELD, :].astype(F32)
        out_ref[...] = jnp.zeros_like(out_ref)

    def two(n, carry):
        at = [step * per_step + 2 * n + i for i in range(2)]
        picked = pair(*[cells[place_of(cols_ref[0, 0, a]), :].astype(BF16) for a in at])
        both = jnp.concatenate([blocks_ref[2 * n], blocks_ref[2 * n + 1]], axis=1)
        value = lax.dot_general(picked, both, (((1,), (1,)), ((), ())), preferred_element_type=F32)
        for i, a in enumerate(at):
            row = rows_ref[0, 0, a]
            out_ref[row] = out_ref[row] + value[8 * i:8 * i + 8] * factor_of(scale_ref[0, 0, a])
        return carry

    lax.fori_loop(0, per_step // 2, two, 0, unroll=8)


def adjoint_kernel(per_step, rows_ref, cols_ref, scale_ref, values_ref, blocks_ref, out_ref, total):
    step = pl.program_id(0)

    @pl.when(step == 0)
    def _():
        total[...] = jnp.zeros_like(total)

    def two(n, carry):
        at = [step * per_step + 2 * n + i for i in range(2)]
        pulled = jnp.concatenate([values_ref[rows_ref[0, 0, a]] for a in at], axis=0)
        both = jnp.concatenate([blocks_ref[2 * n], blocks_ref[2 * n + 1]], axis=1)
        value = jnp.dot(pulled, both, preferred_element_type=F32)
        for i, a in enumerate(at):
            place = place_of(cols_ref[0, 0, a])
            part = value[8 * i:8 * i + 8, EDGE * i:EDGE * i + EDGE]
            total[place, :] = total[place, :] + part * factor_of(scale_ref[0, 0, a])
        return carry

    lax.fori_loop(0, per_step // 2, two, 0, unroll=8)

    @pl.when(step == pl.num_programs(0) - 1)
    def _():
        for k in range(8):
            out_ref[k * FIELD:(k + 1) * FIELD, :] = total[k * STEP:k * STEP + FIELD, :]


def sum_bands_kernel(bands, part_ref, weight_ref, out_ref, got, shard, send, recv, send2, recv2):
    l = lax.axis_index("lat")
    share = part_ref.shape[0] // bands
    greet([{"lat": (l + d) % bands} for d in range(1, bands)])
    mine = pl.ds(l * share, share)

    def first(d):
        peer = (l + d) % bands
        return pltpu.make_async_remote_copy(
            src_ref=part_ref.at[pl.ds(peer * share, share)], dst_ref=got.at[d], send_sem=send.at[d], recv_sem=recv.at[d],
            device_id={"lat": peer}, device_id_type=MESH,
        )

    def second(d, owner):
        return pltpu.make_async_remote_copy(
            src_ref=shard, dst_ref=out_ref.at[pl.ds(owner * share, share)], send_sem=send2.at[d], recv_sem=recv2.at[d],
            device_id={"lat": (l + d) % bands}, device_id_type=MESH,
        )

    for d in range(1, bands):
        first(d).start()
    total = part_ref[mine]
    for d in range(1, bands):
        first(d).wait_recv()
        total = total + got[d]
    weight = weight_ref[mine]
    shard[...] = (total * weight).astype(shard.dtype)
    for d in range(1, bands):
        second(d, l).start()
    out_ref[mine] = shard[...]
    for d in range(1, bands):
        second(d, (l + bands - d) % bands).wait_recv()
    for d in range(1, bands):
        first(d).wait_send()
        second(d, l).wait_send()


def image_kernel(sizes, part_ref, lat_ref, lon_ref, residual_ref, direction_ref, out_ref, coef_ref, own, there, far_out, near_out,
                 relay_out, far_in, near_in, relay_in, mine, band, halo, shard, everyone, res, dire, sums, line_got, line_sum,
                 send, recv, hsend, hrecv, psend, precv, rsend, rrecv, lsend, lrecv, load, local, fields, leave):
    o, l = lax.axis_index("obs"), lax.axis_index("lat")
    bands, weeks, count, bits, lat_decay, lon_decay = sizes
    z, c, at = obs_peers(o)
    partner, up, down = {"obs": at(0, 1 - c)}, {"obs": at(1, c)}, {"obs": at(-1, c)}
    k, side = 2 * CHIPS, CHIPS
    x, y = l // side, l % side
    lines = [[{"lat": x * side + (y + d) % side} for d in range(1, side)], [{"lat": (x + d) % side * side + y} for d in range(1, side)]]
    gets = [pltpu.make_async_copy(residual_ref, res, fields.at[0]), pltpu.make_async_copy(direction_ref, dire, fields.at[1])]
    greet([partner, up, down, {"lat": (l + 1) % bands}, {"lat": (l + bands - 1) % bands}, *lines[0], *lines[1]])
    order = (0, 2, 1, 3)

    def rows_for(core, w):
        return part_ref.at[:, core, w]

    swaps = [remote(rows_for(1 - c, w), there.at[w], (psend, precv), w, partner) for w in range(weeks)]
    loads = [pltpu.make_async_copy(rows_for(c, w), own.at[w], load.at[w]) for w in range(weeks)]
    for w in order:
        swaps[w].start()
        loads[w].start()
    for one in gets:
        one.start()
    sums[...] = jnp.zeros_like(sums)
    lon_width = down_rows(lon_ref, l * BAND)
    weights = lat_rows(lat_ref, lat_decay, l, bands, True)
    ring = (rsend, rrecv)

    def way(w):
        return (1, up, down) if w < 2 else (-1, down, up)

    far = [remote(far_out.at[w], far_in.at[w], ring, (0, w), way(w)[1]) for w in range(weeks)]
    relayed = [remote(relay_out.at[w], relay_in.at[w], ring, (1, w), way(w)[1]) for w in range(weeks)]
    near = [remote(near_out.at[w], near_in.at[w], ring, (2, w), way(w)[2]) for w in range(weeks)]
    halos = [halo_copies(band, halo, w, l, bands, (hsend, hrecv)) for w in range(weeks)]

    def chip_sum(w, step):
        there_too = (z + step + CHIPS) % CHIPS
        return [x + y for x, y in zip(blocks_of(own.at[w, there_too], count), blocks_of(there.at[w, there_too], count))]

    def plus(x, y):
        return [a + d for a, d in zip(x, y)]

    for w in order:
        swaps[w].wait_recv()
        loads[w].wait()
        encode(far_out.at[w], chip_sum(w, 2))
        far[w].start()
        encode(near_out.at[w], chip_sum(w, -way(w)[0]))
        near[w].start()
    gets[0].wait()
    for w in (0, 1):
        gram_first(k, count, w, res, sums)
    for w in order:
        far[w].wait_recv()
        encode(relay_out.at[w], plus(chip_sum(w, way(w)[0]), decode(far_in.at[w], count)))
        relayed[w].start()
    for w in order:
        if w == order[0]:
            for early in (2, 3):
                gram_first(k, count, early, res, sums)
            gets[1].wait()
        near[w].wait_recv()
        relayed[w].wait_recv()
        total = plus(plus(chip_sum(w, 0), decode(near_in.at[w], count)), decode(relay_in.at[w], count))
        encode(band.at[w], total)
        for one in halos[w]:
            one.start()
        put_blocks(mine.at[w], total)

    def produce(w):
        for one in halos[w]:
            one.wait_recv()
        stacks = stacks_of(decode(halo.at[0, w], count), blocks_of(mine.at[w], count), decode(halo.at[1, w], count))
        encode(shard.at[w], along_lon(mix_rows(weights, stacks), lon_width, lon_decay, bits))

    leaving = [pltpu.make_async_copy(everyone.at[:, w], out_ref.at[:, w], leave.at[w]) for w in range(weeks)]

    def consume(w):
        leaving[w].start()
        gram_week(k, count, w, res, dire, everyone, sums)

    run_gather(Gather(shard, everyone, o, (send, recv), local), order, produce, consume)
    total = gram_total(k, sums)
    for axis, here in ((0, y), (1, x)):
        line_sum[axis] = total
        copies = [remote(line_sum.at[axis], line_got.at[axis, here], (lsend, lrecv), (axis, d), to) for d, to in enumerate(lines[axis])]
        for one in copies:
            one.start()
        line_got[axis, here] = total
        for d in range(side - 1):
            back = (here + side - 1 - d) % side
            remote(line_sum.at[axis], line_got.at[axis, back], (lsend, lrecv), (axis, d), lines[axis][d]).wait_recv()
        total = line_got[axis, 0] + line_got[axis, 1] + line_got[axis, 2] + line_got[axis, 3]
        for one in copies:
            one.wait_send()
    coef_ref[...] = coefficients(total)
    for w in range(weeks):
        leaving[w].wait()
        for one in (swaps[w], far[w], relayed[w], near[w], *halos[w]):
            one.wait_send()


def change_block(change_ref, i, w, b, first, rows):
    at = b * BAND + first
    at = at if isinstance(at, int) else pl.multiple_of(at, 16)
    power = change_ref[i, w, WEEK:CODED, :].astype(jnp.int32).astype(F32)
    pick = jnp.sum(jnp.where(iota((16, EDGE), 0) == b, power, 0.0), axis=0, keepdims=True)
    return change_ref[i, w, pl.ds(at, rows), :].astype(jnp.int32).astype(F32) * (jnp.exp2(pick) * (1.0 / TOP))


def add_gram(sums, t, i, j, x, y):
    sums[t, i, j] = sums[t, i, j] + jnp.sum((x * y).reshape(BAND // 8, 8, EDGE), axis=0)


def lanes_of(b):
    return pl.ds(pl.multiple_of(b * EDGE, EDGE), EDGE)


def gram_first(k, count, w, res_ref, sums):
    def one(b, carry):
        res = [res_ref[i, w, :, lanes_of(b)] for i in range(k)]
        for i in range(k):
            for j in range(i, k):
                add_gram(sums, 0, i, j, res[i], res[j])
        return carry

    lax.fori_loop(0, count, one, 0)


def gram_week(k, count, w, res_ref, dire_ref, change_ref, sums):
    def one(b, carry):
        res = [res_ref[i, w, :, lanes_of(b)] for i in range(k)]
        dire = [dire_ref[i, w, :, lanes_of(b)] for i in range(k)]
        img = [dire[i] + change_block(change_ref, i, w, b, 0, BAND) for i in range(k)]
        for i in range(k):
            for j in range(k):
                if i <= j:
                    add_gram(sums, 3, i, j, img[i], img[j])
                add_gram(sums, 1, i, j, dire[i], img[j])
                add_gram(sums, 2, i, j, img[i], res[j])
        return carry

    lax.fori_loop(0, count, one, 0)


def gram_total(k, sums):
    lane = iota((k, EDGE), 1)
    result = jnp.zeros((k, EDGE), F32)
    for t in range(4):
        for i in range(k):
            line = jnp.sum(jnp.sum(sums[t, i], axis=1), axis=1, keepdims=True)
            result = jnp.where(lane == t * k + i, jnp.broadcast_to(line, (k, EDGE)), result)
    return result


def flip(x):
    square = jnp.concatenate([x, jnp.zeros((EDGE - 8, EDGE), F32)], axis=0)
    return jnp.transpose(square)[:8, :]


def product(x, y):
    return sum(jnp.broadcast_to(x[:, i:i + 1], (8, EDGE)) * jnp.broadcast_to(y[i:i + 1, :], (8, EDGE)) for i in range(8))


def solve(a, b):
    row = iota((8, EDGE), 0)
    for p in range(8):
        line = jnp.broadcast_to(a[p:p + 1, :], (8, EDGE))
        line_b = jnp.broadcast_to(b[p:p + 1, :], (8, EDGE))
        column = jnp.broadcast_to(a[:, p:p + 1], (8, EDGE))
        inverse = 1.0 / jnp.broadcast_to(a[p:p + 1, p:p + 1], (8, EDGE))
        ratio = column * inverse
        here = row == p
        a = jnp.where(here, line * inverse, a - ratio * line)
        b = jnp.where(here, line_b * inverse, b - ratio * line_b)
    return b


def coefficients(total):
    lane, row = iota((8, EDGE), 1), iota((8, EDGE), 0)
    parts = []
    for t in range(4):
        moved = total if t == 0 else pltpu.roll(total, EDGE - 8 * t, 1)
        parts.append(jnp.where(lane < 8, moved, 0.0))

    def full(x):
        low = jnp.where(lane <= row, x, 0.0)
        return low + flip(jnp.where(lane < row, x, 0.0))

    gram_old, image_image = full(parts[0]), full(parts[3])
    curvature = 0.5 * (parts[1] + flip(parts[1]))
    residual_image = parts[2]
    step = solve(curvature, gram_old)
    cross = product(residual_image, step)
    gram_new = gram_old - cross - flip(cross) + product(flip(step), product(image_image, step))
    turn = solve(gram_old, gram_new)
    return jnp.where(lane < 8, step, 0.0) + pltpu.roll(jnp.where(lane < 8, turn, 0.0), 8, 1)


def update_kernel(k, coef_ref, solution_ref, residual_ref, direction_ref, change_ref, sol_out, res_out, dir_out):
    rows_each = 32

    def one(b, carry):
        lanes = pl.ds(pl.multiple_of(b * EDGE, EDGE), EDGE)
        for r in range(BAND // rows_each):
            rows = slice(r * rows_each, (r + 1) * rows_each)
            dire = [direction_ref[i, 0, rows, lanes] for i in range(k)]
            more = [change_block(change_ref, i, 0, b, r * rows_each, rows_each) for i in range(k)]
            for a in range(k):
                forth = sum(coef_ref[i, a] * dire[i] for i in range(k))
                back = sum(coef_ref[i, a] * more[i] for i in range(k))
                turn = sum(coef_ref[i, k + a] * dire[i] for i in range(k))
                left = residual_ref[a, 0, rows, lanes] - (forth + back)
                sol_out[a, 0, rows, lanes] = solution_ref[a, 0, rows, lanes] + forth
                res_out[a, 0, rows, lanes] = left
                dir_out[a, 0, rows, lanes] = left + turn
        return carry

    lax.fori_loop(0, 5, one, 0)


def params(collective=None, limit=None):
    extra = {} if collective is None else {"collective_id": collective, "has_side_effects": True}
    return pltpu.CompilerParams(vmem_limit_bytes=limit or (48 << 20), **extra)


def shards(bands, footprints, block_rows, block_cols, block_scale, lat_width, lon_width, obs_weight, solution, residual, direction):
    k, weeks, band_rows, nlon = direction.shape
    blocks = footprints.shape[2]
    count = nlon // EDGE
    assert (k, weeks, band_rows, count, bands) == (8, 4, BAND, 5, CHIPS * CHIPS)
    row_blocks = obs_weight.shape[0] // EDGE
    sizes = (bands, weeks, count, (nlon // 8 + 1).bit_length(), band_rows / 2.0, nlon / 32.0)
    all_rows = k * weeks * WEEK
    plain, coded = (weeks, WEEK, EDGE), (weeks, CODED, EDGE)
    ints = jnp.int16

    cells = pl.pallas_call(
        functools.partial(spread_kernel, sizes),
        out_shape=jax.ShapeDtypeStruct((k, *plain), BF16),
        in_specs=[ANY_SPEC, SMEM_SPEC, SMEM_SPEC],
        out_specs=ANY_SPEC,
        scratch_shapes=[
            VMEM((weeks, band_rows, nlon), F32), VMEM(plain, F32), VMEM(coded, ints), VMEM((2, *coded), ints), VMEM(plain, BF16),
            DMA((7, weeks)), DMA((7, weeks)), DMA((2, weeks)), DMA((2, weeks)), DMA((weeks,)), DMA((weeks,)),
        ],
        compiler_params=params(1, 64_450_000),
        name="spread",
    )(direction, lat_width, lon_width)

    per_step = 64
    smem = [SMEM_SPEC] * 3
    block_spec = pl.BlockSpec((None, None, per_step, EDGE, EDGE), lambda i: (0, 0, i, 0, 0))
    forward = pl.pallas_call(
        functools.partial(forward_kernel, per_step),
        grid=(blocks // per_step,),
        out_shape=jax.ShapeDtypeStruct((row_blocks, k, EDGE), F32),
        in_specs=smem + [pl.BlockSpec((all_rows, EDGE), lambda i: (0, 0)), block_spec],
        out_specs=pl.BlockSpec((row_blocks, k, EDGE), lambda i: (0, 0, 0)),
        scratch_shapes=[VMEM((k * STEP, EDGE), F32)],
        compiler_params=params(None, 66_000_000),
        name="forward",
    )(block_rows, block_cols, block_scale, cells.reshape(all_rows, EDGE), footprints)

    share = row_blocks // bands
    values = pl.pallas_call(
        functools.partial(sum_bands_kernel, bands),
        out_shape=jax.ShapeDtypeStruct((row_blocks, k, EDGE), BF16),
        in_specs=[VMEM_SPEC, VMEM_SPEC],
        out_specs=VMEM_SPEC,
        scratch_shapes=[
            VMEM((bands, share, k, EDGE), F32), VMEM((share, k, EDGE), BF16),
            DMA((bands,)), DMA((bands,)), DMA((bands,)), DMA((bands,)),
        ],
        compiler_params=params(2),
        name="sum_bands",
    )(forward, obs_weight.reshape(row_blocks, 1, EDGE))

    part = pl.pallas_call(
        functools.partial(adjoint_kernel, per_step),
        grid=(blocks // per_step,),
        out_shape=jax.ShapeDtypeStruct((all_rows, EDGE), F32),
        in_specs=smem + [pl.BlockSpec((row_blocks, k, EDGE), lambda i: (0, 0, 0)), block_spec],
        out_specs=pl.BlockSpec((all_rows, EDGE), lambda i: (0, 0)),
        scratch_shapes=[VMEM((k * STEP, EDGE), F32)],
        compiler_params=params(),
        name="adjoint",
    )(block_rows, block_cols, block_scale, values, footprints)

    side = CHIPS
    change, coef = pl.pallas_call(
        functools.partial(image_kernel, sizes),
        out_shape=[jax.ShapeDtypeStruct((k, *coded), ints), jax.ShapeDtypeStruct((k, EDGE), F32)],
        in_specs=[ANY_SPEC, SMEM_SPEC, SMEM_SPEC, ANY_SPEC, ANY_SPEC],
        out_specs=[ANY_SPEC, VMEM_SPEC],
        scratch_shapes=[
            VMEM((weeks, CHIPS, WEEK, EDGE), F32), VMEM((weeks, CHIPS, WEEK, EDGE), F32),
            *[VMEM(coded, ints)] * 6, VMEM(plain, F32), VMEM(coded, ints), VMEM((2, *coded), ints), VMEM(coded, ints),
            VMEM((k, *coded), ints), VMEM(direction.shape, F32), VMEM(direction.shape, F32), VMEM((4, k, k, 8, EDGE), F32),
            VMEM((2, side, k, EDGE), F32), VMEM((2, k, EDGE), F32),
            DMA((7, weeks)), DMA((7, weeks)), DMA((2, weeks)), DMA((2, weeks)), DMA((weeks,)), DMA((weeks,)),
            DMA((3, weeks)), DMA((3, weeks)), DMA((2, side - 1)), DMA((2, side - 1)), DMA((weeks,)), DMA((weeks,)),
            DMA((2,)), DMA((weeks,)),
        ],
        compiler_params=params(3),
        name="image",
    )(part.reshape(CHIPS, 2, *plain), lat_width, lon_width, residual, direction)

    native = pl.BlockSpec((k, 1, band_rows, nlon), lambda w: (0, w, 0, 0))
    packed = pl.BlockSpec((k, 1, CODED, EDGE), lambda w: (0, w, 0, 0))
    return pl.pallas_call(
        functools.partial(update_kernel, k),
        grid=(weeks,),
        out_shape=[jax.ShapeDtypeStruct(direction.shape, F32)] * 3,
        in_specs=[SMEM_SPEC, native, native, native, packed],
        out_specs=[native] * 3,
        compiler_params=params(),
        name="update",
    )(coef, solution, residual, direction, change)


def solution(mesh):
    assert mesh.shape["obs"] == 2 * CHIPS
    three = (P(None, None, "lat", None),) * 3
    blocks = P("obs", "lat", None)
    return jax.shard_map(
        functools.partial(shards, mesh.shape["lat"]),
        mesh=mesh,
        in_specs=(P("obs", "lat", None, None, None), blocks, blocks, blocks, P(), P(), P("obs"), *three),
        out_specs=three,
        check_vma=False,
    )
```

```python
import functools

import jax
import jax.numpy as jnp
from jax import lax
from jax.experimental import pallas as pl
from jax.experimental.pallas import tpu as pltpu
from jax.sharding import PartitionSpec as P

MESH = pl.DeviceIdType.MESH
HIGHEST = lax.Precision.HIGHEST
F32 = jnp.float32
BF16 = jnp.bfloat16
VMEM = pltpu.VMEM
DMA = pltpu.SemaphoreType.DMA
EDGE = 128
CHIPS = 4
ANY_SPEC = pl.BlockSpec(memory_space=pl.ANY)
VMEM_SPEC = pl.BlockSpec(memory_space=pltpu.VMEM)
SMEM_SPEC = pl.BlockSpec(memory_space=pltpu.SMEM)
BAND = 32
WEEK = 160
CODED = WEEK + 16
FIELD = 640
STEP = FIELD + 1
TOP = 32000.0


def iota(shape, axis):
    return lax.broadcasted_iota(jnp.int32, shape, axis)


def norm_of(width, decay):
    p = jnp.exp(jnp.full_like(width, -2.0 / decay))
    return jnp.sqrt(1.0 + 2.0 * p * (1.0 - jnp.exp(width * (-2.0 / decay))) / (1.0 - p))


def down_rows(ref, first):
    row = iota((BAND, EDGE), 0)
    result = jnp.zeros((BAND, EDGE), jnp.int32)
    for r in range(BAND):
        result = jnp.where(row == r, ref[first + r], result)
    return result.astype(F32)


def along_lanes(ref, first, count):
    lane = iota((1, EDGE), 1)
    result = jnp.zeros((1, EDGE), jnp.int32)
    for c in range(count):
        result = jnp.where(lane == c, ref[(first + c) % ref.shape[0]], result)
    return result.astype(F32)


def along_lon(blocks, width, decay, bits):
    rows = blocks[0].shape[0]
    count = len(blocks)
    lane = iota((rows, EDGE), 1)
    terms = width.astype(jnp.int32) + 1
    picks = [((terms >> m) & 1) == 1 for m in range(bits)]

    def shifted(values, step, sign):
        turned = [pltpu.roll(v, step if sign > 0 else EDGE - step, 1) for v in values]
        inside = lane >= step if sign > 0 else lane < EDGE - step
        return [jnp.where(inside, turned[b], turned[(b - sign) % count]) for b in range(count)]

    sides = []
    for sign in (1, -1):
        power = blocks
        total = [jnp.where(picks[0], v, 0.0) for v in blocks]
        for m in range(1, bits):
            half = 2 ** (m - 1)
            moved = shifted(power, half, sign)
            fade = jnp.exp(jnp.full((rows, EDGE), -half / decay, F32))
            power = [a + fade * c for a, c in zip(power, moved)]
            moved = shifted(total, 2 * half, sign)
            fade = fade * fade
            total = [jnp.where(picks[m], a + fade * c, t) for a, c, t in zip(power, moved, total)]
        sides.append(total)
    scale = 1.0 / norm_of(width, decay)
    return [(up + down - x) * scale for up, down, x in zip(sides[0], sides[1], blocks)]


def lat_rows(widths, reach, l, bands, across):
    r, c = iota((BAND, EDGE), 0), iota((BAND, EDGE), 1)
    width = along_lanes(widths, (l + bands - 1) * BAND, 3 * BAND) if across else down_rows(widths, l * BAND)
    distance = jnp.abs(r - c + BAND).astype(F32)
    low = jnp.where(l > 0, 0, BAND)
    high = jnp.where(l < bands - 1, 3 * BAND, 2 * BAND)
    value = jnp.exp(-distance / reach) / norm_of(width, reach)
    return jnp.where((distance <= width) & (c >= low) & (c < high), value, 0.0)


def mix_rows(weights, stacks):
    weights = weights[:, :3 * BAND]
    large = weights.astype(BF16)
    both = jnp.concatenate([large, (weights - large.astype(F32)).astype(BF16)], axis=0)
    stack = jnp.concatenate(stacks, axis=1)
    first = stack.astype(BF16)
    second = (stack - first.astype(F32)).astype(BF16)
    main = jnp.dot(both, first, preferred_element_type=F32)
    total = main[:BAND] + (main[BAND:] + jnp.dot(large, second, preferred_element_type=F32))
    return [total[:, b * EDGE:(b + 1) * EDGE] for b in range(len(stacks))]


def encode(ref, blocks):
    row = iota((16, EDGE), 0)
    powers = jnp.zeros((16, EDGE), F32)
    for b, value in enumerate(blocks):
        top = jnp.max(jnp.abs(value), axis=0, keepdims=True)
        power = jnp.ceil(jnp.log2(jnp.maximum(top, 1e-30)))
        whole = jnp.round(value * (jnp.exp2(-power) * TOP))
        ref[b * BAND:(b + 1) * BAND, :] = whole.astype(jnp.int32).astype(jnp.int16)
        powers = jnp.where(row == b, jnp.broadcast_to(power, (16, EDGE)), powers)
    ref[WEEK:CODED, :] = powers.astype(jnp.int32).astype(jnp.int16)


def scales_of(ref, count):
    powers = jnp.exp2(ref[WEEK:CODED, :].astype(jnp.int32).astype(F32)) * (1.0 / TOP)
    return [powers[b:b + 1, :] for b in range(count)]


def decode(ref, count):
    scales = scales_of(ref, count)
    return [ref[b * BAND:(b + 1) * BAND, :].astype(jnp.int32).astype(F32) * scales[b] for b in range(count)]


def greet(peers):
    barrier = pltpu.get_barrier_semaphore()
    for peer in peers:
        pl.semaphore_signal(barrier, inc=1, device_id=peer, device_id_type=MESH)
    pl.semaphore_wait(barrier, len(peers))


def obs_peers(o):
    z, c = o // 2, o % 2

    def at(step, core):
        return ((z + step + CHIPS) % CHIPS) * 2 + core

    return z, c, at


def remote(src, dst, sems, at, to):
    send, recv = sems
    return pltpu.make_async_remote_copy(
        src_ref=src, dst_ref=dst, send_sem=send.at[at], recv_sem=recv.at[at], device_id=to, device_id_type=MESH,
    )


class Gather:
    def __init__(self, own_ref, out_ref, o, sems, local):
        self.own, self.out, self.o, self.sems = own_ref, out_ref, o, sems
        self.z, self.c, self.at = obs_peers(o)
        self.partner, self.up, self.down = ({"obs": self.at(*p)} for p in ((0, 1 - self.c), (1, self.c), (-1, self.c)))
        self.weeks = own_ref.shape[0]
        self.keep = [pltpu.make_async_copy(own_ref.at[w], out_ref.at[o, w], local.at[w]) for w in range(self.weeks)]
        self.started = []

    def copy(self, role, w, step, core, to):
        ref = self.out.at[self.at(step, core), w]
        return remote(self.own.at[w] if role < 3 else ref, self.out.at[self.o, w] if role < 3 else ref, self.sems, (role, w), to)

    def arrival(self, role, w, step, core):
        ref = self.out.at[self.at(step, core), w]
        remote(self.own.at[w], ref, self.sems, (role, w), self.partner).wait_recv()

    def start(self, *copies):
        for one in copies:
            one.start()
        self.started += copies

    def far_way(self, w):
        return (3, -1, self.up) if w < 2 else (3, 1, self.down)

    def send(self, w):
        self.start(self.copy(1, w, 0, self.c, self.up), self.copy(2, w, 0, self.c, self.down), self.copy(0, w, 0, self.c, self.partner))
        self.keep[w].start()

    def forward(self, w):
        for role, step in ((1, -1), (2, 1)) if w < 2 else ((2, 1), (1, -1)):
            self.arrival(role, w, step, self.c)
            far, far_step, way = self.far_way(w)
            if step == far_step:
                self.start(self.copy(far, w, step, self.c, way))
            self.start(self.copy(3 + role, w, step, self.c, self.partner))

    def relay(self, w):
        self.arrival(3, w, 2, self.c)
        self.start(self.copy(6, w, 2, self.c, self.partner))

    def complete(self, w):
        for role, step in ((0, 0), (4, -1), (5, 1), (6, 2)):
            self.arrival(role, w, step, 1 - self.c)
        self.keep[w].wait()

    def finish(self):
        for one in self.started:
            one.wait_send()


def run_gather(gather, order, produce, consume):
    def finish_week(w):
        gather.complete(w)
        consume(w)

    a, b, c, d = order
    for w, late in ((a, None), (b, None), (c, a), (d, b)):
        produce(w)
        gather.send(w)
        if late is not None:
            gather.forward(late)
    gather.forward(c)
    gather.relay(a)
    gather.forward(d)
    gather.relay(b)
    finish_week(a)
    gather.relay(c)
    gather.relay(d)
    for w in (b, c, d):
        finish_week(w)
    gather.finish()


def halo_copies(src_ref, halo_ref, w, l, bands, sems):
    return [
        remote(src_ref.at[w], halo_ref.at[slot, w], sems, (slot, w), {"lat": (l + step) % bands})
        for slot, step in ((0, 1), (1, bands - 1))
    ]


def stacks_of(low, mid, high):
    return [jnp.concatenate(three, axis=0) for three in zip(low, mid, high)]


def blocks_of(ref, count):
    return [ref[b * BAND:(b + 1) * BAND, :] for b in range(count)]


def put_blocks(ref, blocks):
    for b, value in enumerate(blocks):
        ref[b * BAND:(b + 1) * BAND, :] = value.astype(ref.dtype)


def spread_kernel(sizes, direction_ref, lat_ref, lon_ref, out_ref, field, smooth, wire, halo, shard, send, recv, hsend, hrecv, load, local):
    o, l = lax.axis_index("obs"), lax.axis_index("lat")
    bands, weeks, count, bits, lat_decay, lon_decay = sizes
    loads = [pltpu.make_async_copy(direction_ref.at[o, w], field.at[w], load.at[w]) for w in range(weeks)]
    for one in loads:
        one.start()
    z, c, at = obs_peers(o)
    greet([{"obs": at(0, 1 - c)}, {"obs": at(1, c)}, {"obs": at(-1, c)},
           {"lat": (l + 1) % bands}, {"lat": (l + bands - 1) % bands}])
    lon_width = down_rows(lon_ref, l * BAND)
    weights = lat_rows(lat_ref, lat_decay, l, bands, False)
    halos = []

    def begin(w):
        loads[w].wait()
        done = along_lon([field[w, :, b * EDGE:(b + 1) * EDGE] for b in range(count)], lon_width, lon_decay, bits)
        encode(wire.at[w], done)
        halos.append(halo_copies(wire, halo, w, l, bands, (hsend, hrecv)))
        for one in halos[w]:
            one.start()
        put_blocks(smooth.at[w], done)

    begin(0)
    begin(1)

    def produce(w):
        if w + 2 < weeks:
            begin(w + 2)
        for one in halos[w]:
            one.wait_recv()
        stacks = stacks_of(decode(halo.at[0, w], count), blocks_of(smooth.at[w], count), decode(halo.at[1, w], count))
        put_blocks(shard.at[w], mix_rows(weights, stacks))

    run_gather(Gather(shard, out_ref, o, (send, recv), local), range(weeks), produce, lambda w: None)
    for pair_of in halos:
        for one in pair_of:
            one.wait_send()


def pair(first, second):
    none = jnp.zeros_like(first)
    return jnp.concatenate([jnp.concatenate([first, none], axis=1), jnp.concatenate([none, second], axis=1)], axis=0)


def place_of(col):
    row = (col * 6554) >> 15
    return pl.ds((row >> 5) * WEEK + (col - 5 * row) * BAND + (row & 31), 8, stride=STEP)


def factor_of(scale):
    return (8 >> scale).astype(F32) * 0.125


CHUNK = 32


def all_pairs(blocks_ref, held, sems, two, before=None):
    chunks = held.shape[0] // CHUNK

    def fetch(i):
        some = pl.ds(i * CHUNK, CHUNK)
        return pltpu.make_async_copy(blocks_ref.at[0, 0, some], held.at[some], sems.at[i])

    for i in range(chunks):
        fetch(i).start()
    before()

    def chunk(i, carry):
        fetch(i).wait()
        return lax.fori_loop(0, CHUNK // 2, lambda n, c: two(i * (CHUNK // 2) + n, c), carry, unroll=8)

    lax.fori_loop(0, chunks, chunk, 0)


def forward_kernel(rows_ref, cols_ref, scale_ref, cells_ref, blocks_ref, out_ref, cells, held, sems):
    def before():
        for k in range(8):
            cells[k * STEP:k * STEP + FIELD, :] = cells_ref[k * FIELD:(k + 1) * FIELD, :].astype(F32)
        out_ref[...] = jnp.zeros_like(out_ref)

    def two(n, carry):
        at = [2 * n + i for i in range(2)]
        picked = pair(*[cells[place_of(cols_ref[0, 0, a]), :].astype(BF16) for a in at])
        both = jnp.concatenate([held[a] for a in at], axis=1)
        value = lax.dot_general(picked, both, (((1,), (1,)), ((), ())), preferred_element_type=F32)
        for i, a in enumerate(at):
            row = rows_ref[0, 0, a]
            out_ref[row] = out_ref[row] + value[8 * i:8 * i + 8] * factor_of(scale_ref[0, 0, a])
        return carry

    all_pairs(blocks_ref, held, sems, two, before)


def adjoint_kernel(rows_ref, cols_ref, scale_ref, values_ref, blocks_ref, out_ref, total, held, sems):
    def before():
        total[...] = jnp.zeros_like(total)

    def two(n, carry):
        at = [2 * n + i for i in range(2)]
        pulled = jnp.concatenate([values_ref[rows_ref[0, 0, a]] for a in at], axis=0)
        both = jnp.concatenate([held[a] for a in at], axis=1)
        value = jnp.dot(pulled, both, preferred_element_type=F32)
        for i, a in enumerate(at):
            place = place_of(cols_ref[0, 0, a])
            part = value[8 * i:8 * i + 8, EDGE * i:EDGE * i + EDGE]
            total[place, :] = total[place, :] + part * factor_of(scale_ref[0, 0, a])
        return carry

    all_pairs(blocks_ref, held, sems, two, before)
    for k in range(8):
        out_ref[k * FIELD:(k + 1) * FIELD, :] = total[k * STEP:k * STEP + FIELD, :]


def sum_bands_kernel(bands, part_ref, weight_ref, out_ref, got, shard, send, recv, send2, recv2):
    l = lax.axis_index("lat")
    share = part_ref.shape[0] // bands
    greet([{"lat": (l + d) % bands} for d in range(1, bands)])
    mine = pl.ds(l * share, share)

    def first(d):
        peer = (l + d) % bands
        return pltpu.make_async_remote_copy(
            src_ref=part_ref.at[pl.ds(peer * share, share)], dst_ref=got.at[d], send_sem=send.at[d], recv_sem=recv.at[d],
            device_id={"lat": peer}, device_id_type=MESH,
        )

    def second(d, owner):
        return pltpu.make_async_remote_copy(
            src_ref=shard, dst_ref=out_ref.at[pl.ds(owner * share, share)], send_sem=send2.at[d], recv_sem=recv2.at[d],
            device_id={"lat": (l + d) % bands}, device_id_type=MESH,
        )

    for d in range(1, bands):
        first(d).start()
    total = part_ref[mine]
    for d in range(1, bands):
        first(d).wait_recv()
        total = total + got[d]
    weight = weight_ref[mine]
    shard[...] = (total * weight).astype(shard.dtype)
    for d in range(1, bands):
        second(d, l).start()
    out_ref[mine] = shard[...]
    for d in range(1, bands):
        second(d, (l + bands - d) % bands).wait_recv()
    for d in range(1, bands):
        first(d).wait_send()
        second(d, l).wait_send()


def image_kernel(sizes, part_ref, lat_ref, lon_ref, residual_ref, direction_ref, out_ref, coef_ref, own, there, far_out, near_out,
                 relay_out, far_in, near_in, relay_in, mine, band, halo, shard, everyone, res, dire, sums, line_got, line_sum,
                 send, recv, hsend, hrecv, psend, precv, rsend, rrecv, lsend, lrecv, load, local, fields, leave):
    o, l = lax.axis_index("obs"), lax.axis_index("lat")
    bands, weeks, count, bits, lat_decay, lon_decay = sizes
    z, c, at = obs_peers(o)
    partner, up, down = {"obs": at(0, 1 - c)}, {"obs": at(1, c)}, {"obs": at(-1, c)}
    k, side = 2 * CHIPS, CHIPS
    x, y = l // side, l % side
    lines = [[{"lat": x * side + (y + d) % side} for d in range(1, side)], [{"lat": (x + d) % side * side + y} for d in range(1, side)]]
    gets = [pltpu.make_async_copy(residual_ref, res, fields.at[0]), pltpu.make_async_copy(direction_ref, dire, fields.at[1])]
    greet([partner, up, down, {"lat": (l + 1) % bands}, {"lat": (l + bands - 1) % bands}, *lines[0], *lines[1]])
    order = (0, 2, 1, 3)

    def rows_for(core, w):
        return part_ref.at[:, core, w]

    swaps = [remote(rows_for(1 - c, w), there.at[w], (psend, precv), w, partner) for w in range(weeks)]
    loads = [pltpu.make_async_copy(rows_for(c, w), own.at[w], load.at[w]) for w in range(weeks)]
    for w in order:
        swaps[w].start()
        loads[w].start()
    for one in gets:
        one.start()
    sums[...] = jnp.zeros_like(sums)
    lon_width = down_rows(lon_ref, l * BAND)
    weights = lat_rows(lat_ref, lat_decay, l, bands, True)
    ring = (rsend, rrecv)

    def way(w):
        return (1, up, down) if w < 2 else (-1, down, up)

    far = [remote(far_out.at[w], far_in.at[w], ring, (0, w), way(w)[1]) for w in range(weeks)]
    relayed = [remote(relay_out.at[w], relay_in.at[w], ring, (1, w), way(w)[1]) for w in range(weeks)]
    near = [remote(near_out.at[w], near_in.at[w], ring, (2, w), way(w)[2]) for w in range(weeks)]
    halos = [halo_copies(band, halo, w, l, bands, (hsend, hrecv)) for w in range(weeks)]

    def chip_sum(w, step):
        there_too = (z + step + CHIPS) % CHIPS
        return [x + y for x, y in zip(blocks_of(own.at[w, there_too], count), blocks_of(there.at[w, there_too], count))]

    def plus(x, y):
        return [a + d for a, d in zip(x, y)]

    for w in order:
        swaps[w].wait_recv()
        loads[w].wait()
        encode(far_out.at[w], chip_sum(w, 2))
        far[w].start()
        encode(near_out.at[w], chip_sum(w, -way(w)[0]))
        near[w].start()
    gets[0].wait()
    for w in (0, 1):
        gram_first(k, count, w, res, sums)
    for w in order:
        far[w].wait_recv()
        encode(relay_out.at[w], plus(chip_sum(w, way(w)[0]), decode(far_in.at[w], count)))
        relayed[w].start()
    for w in order:
        if w == order[0]:
            for early in (2, 3):
                gram_first(k, count, early, res, sums)
            gets[1].wait()
        near[w].wait_recv()
        relayed[w].wait_recv()
        total = plus(plus(chip_sum(w, 0), decode(near_in.at[w], count)), decode(relay_in.at[w], count))
        encode(band.at[w], total)
        for one in halos[w]:
            one.start()
        put_blocks(mine.at[w], total)

    def produce(w):
        for one in halos[w]:
            one.wait_recv()
        stacks = stacks_of(decode(halo.at[0, w], count), blocks_of(mine.at[w], count), decode(halo.at[1, w], count))
        encode(shard.at[w], along_lon(mix_rows(weights, stacks), lon_width, lon_decay, bits))

    leaving = [pltpu.make_async_copy(everyone.at[:, w], out_ref.at[:, w], leave.at[w]) for w in range(weeks)]

    def consume(w):
        leaving[w].start()
        gram_week(k, count, w, res, dire, everyone, sums)

    run_gather(Gather(shard, everyone, o, (send, recv), local), order, produce, consume)
    total = gram_total(k, sums)
    for axis, here in ((0, y), (1, x)):
        line_sum[axis] = total
        copies = [remote(line_sum.at[axis], line_got.at[axis, here], (lsend, lrecv), (axis, d), to) for d, to in enumerate(lines[axis])]
        for one in copies:
            one.start()
        line_got[axis, here] = total
        for d in range(side - 1):
            back = (here + side - 1 - d) % side
            remote(line_sum.at[axis], line_got.at[axis, back], (lsend, lrecv), (axis, d), lines[axis][d]).wait_recv()
        total = line_got[axis, 0] + line_got[axis, 1] + line_got[axis, 2] + line_got[axis, 3]
        for one in copies:
            one.wait_send()
    coef_ref[...] = coefficients(total)
    for w in range(weeks):
        leaving[w].wait()
        for one in (swaps[w], far[w], relayed[w], near[w], *halos[w]):
            one.wait_send()


def change_block(change_ref, i, w, b, first, rows):
    at = b * BAND + first
    at = at if isinstance(at, int) else pl.multiple_of(at, 16)
    power = change_ref[i, w, WEEK:CODED, :].astype(jnp.int32).astype(F32)
    pick = jnp.sum(jnp.where(iota((16, EDGE), 0) == b, power, 0.0), axis=0, keepdims=True)
    return change_ref[i, w, pl.ds(at, rows), :].astype(jnp.int32).astype(F32) * (jnp.exp2(pick) * (1.0 / TOP))


def add_gram(sums, t, i, j, x, y):
    sums[t, i, j] = sums[t, i, j] + jnp.sum((x * y).reshape(BAND // 8, 8, EDGE), axis=0)


def lanes_of(b):
    return pl.ds(pl.multiple_of(b * EDGE, EDGE), EDGE)


def gram_first(k, count, w, res_ref, sums):
    def one(b, carry):
        res = [res_ref[i, w, :, lanes_of(b)] for i in range(k)]
        for i in range(k):
            for j in range(i, k):
                add_gram(sums, 0, i, j, res[i], res[j])
        return carry

    lax.fori_loop(0, count, one, 0)


def gram_week(k, count, w, res_ref, dire_ref, change_ref, sums):
    def one(b, carry):
        res = [res_ref[i, w, :, lanes_of(b)] for i in range(k)]
        dire = [dire_ref[i, w, :, lanes_of(b)] for i in range(k)]
        img = [dire[i] + change_block(change_ref, i, w, b, 0, BAND) for i in range(k)]
        for i in range(k):
            for j in range(k):
                if i <= j:
                    add_gram(sums, 3, i, j, img[i], img[j])
                add_gram(sums, 1, i, j, dire[i], img[j])
                add_gram(sums, 2, i, j, img[i], res[j])
        return carry

    lax.fori_loop(0, count, one, 0)


def gram_total(k, sums):
    lane = iota((k, EDGE), 1)
    result = jnp.zeros((k, EDGE), F32)
    for t in range(4):
        for i in range(k):
            line = jnp.sum(jnp.sum(sums[t, i], axis=1), axis=1, keepdims=True)
            result = jnp.where(lane == t * k + i, jnp.broadcast_to(line, (k, EDGE)), result)
    return result


def flip(x):
    square = jnp.concatenate([x, jnp.zeros((EDGE - 8, EDGE), F32)], axis=0)
    return jnp.transpose(square)[:8, :]


def product(x, y):
    return sum(jnp.broadcast_to(x[:, i:i + 1], (8, EDGE)) * jnp.broadcast_to(y[i:i + 1, :], (8, EDGE)) for i in range(8))


def solve(a, b):
    row = iota((8, EDGE), 0)
    for p in range(8):
        line = jnp.broadcast_to(a[p:p + 1, :], (8, EDGE))
        line_b = jnp.broadcast_to(b[p:p + 1, :], (8, EDGE))
        column = jnp.broadcast_to(a[:, p:p + 1], (8, EDGE))
        inverse = 1.0 / jnp.broadcast_to(a[p:p + 1, p:p + 1], (8, EDGE))
        ratio = column * inverse
        here = row == p
        a = jnp.where(here, line * inverse, a - ratio * line)
        b = jnp.where(here, line_b * inverse, b - ratio * line_b)
    return b


def coefficients(total):
    lane, row = iota((8, EDGE), 1), iota((8, EDGE), 0)
    parts = []
    for t in range(4):
        moved = total if t == 0 else pltpu.roll(total, EDGE - 8 * t, 1)
        parts.append(jnp.where(lane < 8, moved, 0.0))

    def full(x):
        low = jnp.where(lane <= row, x, 0.0)
        return low + flip(jnp.where(lane < row, x, 0.0))

    gram_old, image_image = full(parts[0]), full(parts[3])
    curvature = 0.5 * (parts[1] + flip(parts[1]))
    residual_image = parts[2]
    step = solve(curvature, gram_old)
    inverse = solve(gram_old, jnp.where(lane == row, 1.0, 0.0))
    cross = product(residual_image, step)
    gram_new = gram_old - cross - flip(cross) + product(flip(step), product(image_image, step))
    turn = product(inverse, gram_new)
    return jnp.where(lane < 8, step, 0.0) + pltpu.roll(jnp.where(lane < 8, turn, 0.0), 8, 1)


def update_kernel(k, coef_ref, solution_ref, residual_ref, direction_ref, change_ref, sol_out, res_out, dir_out):
    rows_each = 32

    def one(b, carry):
        lanes = pl.ds(pl.multiple_of(b * EDGE, EDGE), EDGE)
        for r in range(BAND // rows_each):
            rows = slice(r * rows_each, (r + 1) * rows_each)
            dire = [direction_ref[i, 0, rows, lanes] for i in range(k)]
            more = [change_block(change_ref, i, 0, b, r * rows_each, rows_each) for i in range(k)]
            for a in range(k):
                forth = sum(coef_ref[i, a] * dire[i] for i in range(k))
                back = sum(coef_ref[i, a] * more[i] for i in range(k))
                turn = sum(coef_ref[i, k + a] * dire[i] for i in range(k))
                left = residual_ref[a, 0, rows, lanes] - (forth + back)
                sol_out[a, 0, rows, lanes] = solution_ref[a, 0, rows, lanes] + forth
                res_out[a, 0, rows, lanes] = left
                dir_out[a, 0, rows, lanes] = left + turn
        return carry

    lax.fori_loop(0, 5, one, 0)


def params(collective=None, limit=None):
    extra = {} if collective is None else {"collective_id": collective, "has_side_effects": True}
    return pltpu.CompilerParams(vmem_limit_bytes=limit or (48 << 20), **extra)


def shards(bands, footprints, block_rows, block_cols, block_scale, lat_width, lon_width, obs_weight, solution, residual, direction):
    k, weeks, band_rows, nlon = direction.shape
    blocks = footprints.shape[2]
    count = nlon // EDGE
    assert (k, weeks, band_rows, count, bands) == (8, 4, BAND, 5, CHIPS * CHIPS)
    row_blocks = obs_weight.shape[0] // EDGE
    sizes = (bands, weeks, count, (nlon // 8 + 1).bit_length(), band_rows / 2.0, nlon / 32.0)
    all_rows = k * weeks * WEEK
    plain, coded = (weeks, WEEK, EDGE), (weeks, CODED, EDGE)
    ints = jnp.int16

    cells = pl.pallas_call(
        functools.partial(spread_kernel, sizes),
        out_shape=jax.ShapeDtypeStruct((k, *plain), BF16),
        in_specs=[ANY_SPEC, SMEM_SPEC, SMEM_SPEC],
        out_specs=ANY_SPEC,
        scratch_shapes=[
            VMEM((weeks, band_rows, nlon), F32), VMEM(plain, F32), VMEM(coded, ints), VMEM((2, *coded), ints), VMEM(plain, BF16),
            DMA((7, weeks)), DMA((7, weeks)), DMA((2, weeks)), DMA((2, weeks)), DMA((weeks,)), DMA((weeks,)),
        ],
        compiler_params=params(1, 64_450_000),
        name="spread",
    )(direction, lat_width, lon_width)

    blocks_held = [VMEM((blocks, EDGE, EDGE), BF16), DMA((blocks // CHUNK,))]
    smem = [SMEM_SPEC] * 3
    forward = pl.pallas_call(
        forward_kernel,
        out_shape=jax.ShapeDtypeStruct((row_blocks, k, EDGE), F32),
        in_specs=smem + [VMEM_SPEC, ANY_SPEC],
        out_specs=VMEM_SPEC,
        scratch_shapes=[VMEM((k * STEP, EDGE), F32), *blocks_held],
        compiler_params=params(),
        name="forward",
    )(block_rows, block_cols, block_scale, cells.reshape(all_rows, EDGE), footprints)

    share = row_blocks // bands
    values = pl.pallas_call(
        functools.partial(sum_bands_kernel, bands),
        out_shape=jax.ShapeDtypeStruct((row_blocks, k, EDGE), BF16),
        in_specs=[VMEM_SPEC, VMEM_SPEC],
        out_specs=VMEM_SPEC,
        scratch_shapes=[
            VMEM((bands, share, k, EDGE), F32), VMEM((share, k, EDGE), BF16),
            DMA((bands,)), DMA((bands,)), DMA((bands,)), DMA((bands,)),
        ],
        compiler_params=params(2),
        name="sum_bands",
    )(forward, obs_weight.reshape(row_blocks, 1, EDGE))

    part = pl.pallas_call(
        adjoint_kernel,
        out_shape=jax.ShapeDtypeStruct((all_rows, EDGE), F32),
        in_specs=smem + [VMEM_SPEC, ANY_SPEC],
        out_specs=VMEM_SPEC,
        scratch_shapes=[VMEM((k * STEP, EDGE), F32), *blocks_held],
        compiler_params=params(),
        name="adjoint",
    )(block_rows, block_cols, block_scale, values, footprints)

    side = CHIPS
    change, coef = pl.pallas_call(
        functools.partial(image_kernel, sizes),
        out_shape=[jax.ShapeDtypeStruct((k, *coded), ints), jax.ShapeDtypeStruct((k, EDGE), F32)],
        in_specs=[ANY_SPEC, SMEM_SPEC, SMEM_SPEC, ANY_SPEC, ANY_SPEC],
        out_specs=[ANY_SPEC, VMEM_SPEC],
        scratch_shapes=[
            VMEM((weeks, CHIPS, WEEK, EDGE), F32), VMEM((weeks, CHIPS, WEEK, EDGE), F32),
            *[VMEM(coded, ints)] * 6, VMEM(plain, F32), VMEM(coded, ints), VMEM((2, *coded), ints), VMEM(coded, ints),
            VMEM((k, *coded), ints), VMEM(direction.shape, F32), VMEM(direction.shape, F32), VMEM((4, k, k, 8, EDGE), F32),
            VMEM((2, side, k, EDGE), F32), VMEM((2, k, EDGE), F32),
            DMA((7, weeks)), DMA((7, weeks)), DMA((2, weeks)), DMA((2, weeks)), DMA((weeks,)), DMA((weeks,)),
            DMA((3, weeks)), DMA((3, weeks)), DMA((2, side - 1)), DMA((2, side - 1)), DMA((weeks,)), DMA((weeks,)),
            DMA((2,)), DMA((weeks,)),
        ],
        compiler_params=params(3),
        name="image",
    )(part.reshape(CHIPS, 2, *plain), lat_width, lon_width, residual, direction)

    native = pl.BlockSpec((k, 1, band_rows, nlon), lambda w: (0, w, 0, 0))
    packed = pl.BlockSpec((k, 1, CODED, EDGE), lambda w: (0, w, 0, 0))
    return pl.pallas_call(
        functools.partial(update_kernel, k),
        grid=(weeks,),
        out_shape=[jax.ShapeDtypeStruct(direction.shape, F32)] * 3,
        in_specs=[SMEM_SPEC, native, native, native, packed],
        out_specs=[native] * 3,
        compiler_params=params(),
        name="update",
    )(coef, solution, residual, direction, change)


def solution(mesh):
    assert mesh.shape["obs"] == 2 * CHIPS
    three = (P(None, None, "lat", None),) * 3
    blocks = P("obs", "lat", None)
    return jax.shard_map(
        functools.partial(shards, mesh.shape["lat"]),
        mesh=mesh,
        in_specs=(P("obs", "lat", None, None, None), blocks, blocks, blocks, P(), P(), P("obs"), *three),
        out_specs=three,
        check_vma=False,
    )
```

```python
import functools

import jax
import jax.numpy as jnp
from jax import lax
from jax.experimental import pallas as pl
from jax.experimental.pallas import tpu as pltpu
from jax.sharding import PartitionSpec as P

MESH = pl.DeviceIdType.MESH
HIGHEST = lax.Precision.HIGHEST
F32 = jnp.float32
BF16 = jnp.bfloat16
VMEM = pltpu.VMEM
DMA = pltpu.SemaphoreType.DMA
EDGE = 128
CHIPS = 4
ANY_SPEC = pl.BlockSpec(memory_space=pl.ANY)
VMEM_SPEC = pl.BlockSpec(memory_space=pltpu.VMEM)
SMEM_SPEC = pl.BlockSpec(memory_space=pltpu.SMEM)
BAND = 32
WEEK = 160
CODED = WEEK + 16
FIELD = 640
STEP = FIELD + 1
TOP = 32000.0


def iota(shape, axis):
    return lax.broadcasted_iota(jnp.int32, shape, axis)


def norm_of(width, decay):
    p = jnp.exp(jnp.full_like(width, -2.0 / decay))
    return jnp.sqrt(1.0 + 2.0 * p * (1.0 - jnp.exp(width * (-2.0 / decay))) / (1.0 - p))


def down_rows(ref, first):
    row = iota((BAND, EDGE), 0)
    result = jnp.zeros((BAND, EDGE), jnp.int32)
    for r in range(BAND):
        result = jnp.where(row == r, ref[first + r], result)
    return result.astype(F32)


def along_lanes(ref, first, count):
    lane = iota((1, EDGE), 1)
    result = jnp.zeros((1, EDGE), jnp.int32)
    for c in range(count):
        result = jnp.where(lane == c, ref[(first + c) % ref.shape[0]], result)
    return result.astype(F32)


def along_lon(blocks, width, decay, bits):
    rows = blocks[0].shape[0]
    count = len(blocks)
    lane = iota((rows, EDGE), 1)
    terms = width.astype(jnp.int32) + 1
    picks = [((terms >> m) & 1) == 1 for m in range(bits)]

    def shifted(values, step, sign):
        turned = [pltpu.roll(v, step if sign > 0 else EDGE - step, 1) for v in values]
        inside = lane >= step if sign > 0 else lane < EDGE - step
        return [jnp.where(inside, turned[b], turned[(b - sign) % count]) for b in range(count)]

    sides = []
    for sign in (1, -1):
        power = blocks
        total = [jnp.where(picks[0], v, 0.0) for v in blocks]
        for m in range(1, bits):
            half = 2 ** (m - 1)
            moved = shifted(power, half, sign)
            fade = jnp.exp(jnp.full((rows, EDGE), -half / decay, F32))
            power = [a + fade * c for a, c in zip(power, moved)]
            moved = shifted(total, 2 * half, sign)
            fade = fade * fade
            total = [jnp.where(picks[m], a + fade * c, t) for a, c, t in zip(power, moved, total)]
        sides.append(total)
    scale = 1.0 / norm_of(width, decay)
    return [(up + down - x) * scale for up, down, x in zip(sides[0], sides[1], blocks)]


def lat_rows(widths, reach, l, bands, across):
    r, c = iota((BAND, EDGE), 0), iota((BAND, EDGE), 1)
    width = along_lanes(widths, (l + bands - 1) * BAND, 3 * BAND) if across else down_rows(widths, l * BAND)
    distance = jnp.abs(r - c + BAND).astype(F32)
    low = jnp.where(l > 0, 0, BAND)
    high = jnp.where(l < bands - 1, 3 * BAND, 2 * BAND)
    value = jnp.exp(-distance / reach) / norm_of(width, reach)
    return jnp.where((distance <= width) & (c >= low) & (c < high), value, 0.0)


def mix_rows(weights, stacks):
    weights = weights[:, :3 * BAND]
    large = weights.astype(BF16)
    both = jnp.concatenate([large, (weights - large.astype(F32)).astype(BF16)], axis=0)
    stack = jnp.concatenate(stacks, axis=1)
    first = stack.astype(BF16)
    second = (stack - first.astype(F32)).astype(BF16)
    main = jnp.dot(both, first, preferred_element_type=F32)
    total = main[:BAND] + (main[BAND:] + jnp.dot(large, second, preferred_element_type=F32))
    return [total[:, b * EDGE:(b + 1) * EDGE] for b in range(len(stacks))]


def encode(ref, blocks):
    row = iota((16, EDGE), 0)
    powers = jnp.zeros((16, EDGE), F32)
    for b, value in enumerate(blocks):
        top = jnp.max(jnp.abs(value), axis=0, keepdims=True)
        power = jnp.ceil(jnp.log2(jnp.maximum(top, 1e-30)))
        whole = jnp.round(value * (jnp.exp2(-power) * TOP))
        ref[b * BAND:(b + 1) * BAND, :] = whole.astype(jnp.int32).astype(jnp.int16)
        powers = jnp.where(row == b, jnp.broadcast_to(power, (16, EDGE)), powers)
    ref[WEEK:CODED, :] = powers.astype(jnp.int32).astype(jnp.int16)


def scales_of(ref, count):
    powers = jnp.exp2(ref[WEEK:CODED, :].astype(jnp.int32).astype(F32)) * (1.0 / TOP)
    return [powers[b:b + 1, :] for b in range(count)]


def decode(ref, count):
    scales = scales_of(ref, count)
    return [ref[b * BAND:(b + 1) * BAND, :].astype(jnp.int32).astype(F32) * scales[b] for b in range(count)]


def greet(peers):
    barrier = pltpu.get_barrier_semaphore()
    for peer in peers:
        pl.semaphore_signal(barrier, inc=1, device_id=peer, device_id_type=MESH)
    pl.semaphore_wait(barrier, len(peers))


def obs_peers(o):
    z, c = o // 2, o % 2

    def at(step, core):
        return ((z + step + CHIPS) % CHIPS) * 2 + core

    return z, c, at


def remote(src, dst, sems, at, to):
    send, recv = sems
    return pltpu.make_async_remote_copy(
        src_ref=src, dst_ref=dst, send_sem=send.at[at], recv_sem=recv.at[at], device_id=to, device_id_type=MESH,
    )


class Gather:
    def __init__(self, own_ref, out_ref, o, sems, local):
        self.own, self.out, self.o, self.sems = own_ref, out_ref, o, sems
        self.z, self.c, self.at = obs_peers(o)
        self.partner, self.up, self.down = ({"obs": self.at(*p)} for p in ((0, 1 - self.c), (1, self.c), (-1, self.c)))
        self.weeks = own_ref.shape[0]
        self.keep = [pltpu.make_async_copy(own_ref.at[w], out_ref.at[o, w], local.at[w]) for w in range(self.weeks)]
        self.started = []

    def copy(self, role, w, step, core, to):
        ref = self.out.at[self.at(step, core), w]
        return remote(self.own.at[w] if role < 3 else ref, self.out.at[self.o, w] if role < 3 else ref, self.sems, (role, w), to)

    def arrival(self, role, w, step, core):
        ref = self.out.at[self.at(step, core), w]
        remote(self.own.at[w], ref, self.sems, (role, w), self.partner).wait_recv()

    def start(self, *copies):
        for one in copies:
            one.start()
        self.started += copies

    def far_way(self, w):
        return (3, -1, self.up) if w < 2 else (3, 1, self.down)

    def send(self, w):
        self.start(self.copy(1, w, 0, self.c, self.up), self.copy(2, w, 0, self.c, self.down), self.copy(0, w, 0, self.c, self.partner))
        self.keep[w].start()

    def forward(self, w):
        for role, step in ((1, -1), (2, 1)) if w < 2 else ((2, 1), (1, -1)):
            self.arrival(role, w, step, self.c)
            far, far_step, way = self.far_way(w)
            if step == far_step:
                self.start(self.copy(far, w, step, self.c, way))
            self.start(self.copy(3 + role, w, step, self.c, self.partner))

    def relay(self, w):
        self.arrival(3, w, 2, self.c)
        self.start(self.copy(6, w, 2, self.c, self.partner))

    def complete(self, w):
        for role, step in ((0, 0), (4, -1), (5, 1), (6, 2)):
            self.arrival(role, w, step, 1 - self.c)
        self.keep[w].wait()

    def finish(self):
        for one in self.started:
            one.wait_send()


def run_gather(gather, order, produce, consume):
    def finish_week(w):
        gather.complete(w)
        consume(w)

    a, b, c, d = order
    for w, late in ((a, None), (b, None), (c, a), (d, b)):
        produce(w)
        gather.send(w)
        if late is not None:
            gather.forward(late)
    gather.forward(c)
    gather.relay(a)
    gather.forward(d)
    gather.relay(b)
    finish_week(a)
    gather.relay(c)
    gather.relay(d)
    for w in (b, c, d):
        finish_week(w)
    gather.finish()


def halo_copies(src_ref, halo_ref, w, l, bands, sems):
    return [
        remote(src_ref.at[w], halo_ref.at[slot, w], sems, (slot, w), {"lat": (l + step) % bands})
        for slot, step in ((0, 1), (1, bands - 1))
    ]


def stacks_of(low, mid, high):
    return [jnp.concatenate(three, axis=0) for three in zip(low, mid, high)]


def blocks_of(ref, count):
    return [ref[b * BAND:(b + 1) * BAND, :] for b in range(count)]


def put_blocks(ref, blocks):
    for b, value in enumerate(blocks):
        ref[b * BAND:(b + 1) * BAND, :] = value.astype(ref.dtype)


def spread_kernel(sizes, direction_ref, lat_ref, lon_ref, out_ref, field, smooth, wire, halo, shard, send, recv, hsend, hrecv, load, local):
    o, l = lax.axis_index("obs"), lax.axis_index("lat")
    bands, weeks, count, bits, lat_decay, lon_decay = sizes
    loads = [pltpu.make_async_copy(direction_ref.at[o, w], field.at[w], load.at[w]) for w in range(weeks)]
    for one in loads:
        one.start()
    z, c, at = obs_peers(o)
    greet([{"obs": at(0, 1 - c)}, {"obs": at(1, c)}, {"obs": at(-1, c)},
           {"lat": (l + 1) % bands}, {"lat": (l + bands - 1) % bands}])
    lon_width = down_rows(lon_ref, l * BAND)
    weights = lat_rows(lat_ref, lat_decay, l, bands, False)
    halos = []

    def begin(w):
        loads[w].wait()
        done = along_lon([field[w, :, b * EDGE:(b + 1) * EDGE] for b in range(count)], lon_width, lon_decay, bits)
        encode(wire.at[w], done)
        halos.append(halo_copies(wire, halo, w, l, bands, (hsend, hrecv)))
        for one in halos[w]:
            one.start()
        put_blocks(smooth.at[w], done)

    begin(0)
    begin(1)

    def produce(w):
        if w + 2 < weeks:
            begin(w + 2)
        for one in halos[w]:
            one.wait_recv()
        stacks = stacks_of(decode(halo.at[0, w], count), blocks_of(smooth.at[w], count), decode(halo.at[1, w], count))
        put_blocks(shard.at[w], mix_rows(weights, stacks))

    run_gather(Gather(shard, out_ref, o, (send, recv), local), range(weeks), produce, lambda w: None)
    for pair_of in halos:
        for one in pair_of:
            one.wait_send()


def pair(first, second):
    none = jnp.zeros_like(first)
    return jnp.concatenate([jnp.concatenate([first, none], axis=1), jnp.concatenate([none, second], axis=1)], axis=0)


def place_of(col):
    row = (col * 6554) >> 15
    return pl.ds((row >> 5) * WEEK + (col - 5 * row) * BAND + (row & 31), 8, stride=STEP)


def factor_of(scale):
    return (8 >> scale).astype(F32) * 0.125


CHUNK = 32


def all_pairs(blocks_ref, held, sems, two, before=None):
    chunks = held.shape[0] // CHUNK

    def fetch(i):
        some = pl.ds(i * CHUNK, CHUNK)
        return pltpu.make_async_copy(blocks_ref.at[0, 0, some], held.at[some], sems.at[i])

    for i in range(chunks):
        fetch(i).start()
    before()

    def chunk(i, carry):
        fetch(i).wait()
        return lax.fori_loop(0, CHUNK // 2, lambda n, c: two(i * (CHUNK // 2) + n, c), carry, unroll=8)

    lax.fori_loop(0, chunks, chunk, 0)


def forward_kernel(rows_ref, cols_ref, scale_ref, cells_ref, blocks_ref, out_ref, cells, held, sems):
    def before():
        for k in range(8):
            cells[k * STEP:k * STEP + FIELD, :] = cells_ref[k * FIELD:(k + 1) * FIELD, :].astype(F32)
        out_ref[...] = jnp.zeros_like(out_ref)

    def two(n, carry):
        at = [2 * n + i for i in range(2)]
        picked = pair(*[cells[place_of(cols_ref[0, 0, a]), :].astype(BF16) for a in at])
        both = jnp.concatenate([held[a] for a in at], axis=1)
        value = lax.dot_general(picked, both, (((1,), (1,)), ((), ())), preferred_element_type=F32)
        for i, a in enumerate(at):
            row = rows_ref[0, 0, a]
            out_ref[row] = out_ref[row] + value[8 * i:8 * i + 8] * factor_of(scale_ref[0, 0, a])
        return carry

    all_pairs(blocks_ref, held, sems, two, before)


def adjoint_kernel(rows_ref, cols_ref, scale_ref, values_ref, blocks_ref, out_ref, total, held, sems):
    def before():
        total[...] = jnp.zeros_like(total)

    def two(n, carry):
        at = [2 * n + i for i in range(2)]
        pulled = jnp.concatenate([values_ref[rows_ref[0, 0, a]] for a in at], axis=0)
        both = jnp.concatenate([held[a] for a in at], axis=1)
        value = jnp.dot(pulled, both, preferred_element_type=F32)
        for i, a in enumerate(at):
            place = place_of(cols_ref[0, 0, a])
            part = value[8 * i:8 * i + 8, EDGE * i:EDGE * i + EDGE]
            total[place, :] = total[place, :] + part * factor_of(scale_ref[0, 0, a])
        return carry

    all_pairs(blocks_ref, held, sems, two, before)
    for k in range(8):
        out_ref[k * FIELD:(k + 1) * FIELD, :] = total[k * STEP:k * STEP + FIELD, :]


def sum_bands_kernel(bands, part_ref, weight_ref, out_ref, got, shard, send, recv, send2, recv2):
    l = lax.axis_index("lat")
    share = part_ref.shape[0] // bands
    far_first = (10, 6, 9, 11, 14, 2, 8, 5, 7, 13, 3, 15, 12, 1, 4)
    greet([{"lat": (l + d) % bands} for d in far_first])
    mine = pl.ds(l * share, share)

    def first(d):
        peer = (l + d) % bands
        return pltpu.make_async_remote_copy(
            src_ref=part_ref.at[pl.ds(peer * share, share)], dst_ref=got.at[d], send_sem=send.at[d], recv_sem=recv.at[d],
            device_id={"lat": peer}, device_id_type=MESH,
        )

    def second(d, owner):
        return pltpu.make_async_remote_copy(
            src_ref=shard, dst_ref=out_ref.at[pl.ds(owner * share, share)], send_sem=send2.at[d], recv_sem=recv2.at[d],
            device_id={"lat": (l + d) % bands}, device_id_type=MESH,
        )

    for d in far_first:
        first(d).start()
    total = part_ref[mine]
    for d in far_first[::-1]:
        first(d).wait_recv()
        total = total + got[d]
    weight = weight_ref[mine]
    shard[...] = (total * weight).astype(shard.dtype)
    for d in far_first:
        second(d, l).start()
    out_ref[mine] = shard[...]
    for d in far_first[::-1]:
        second(d, (l + bands - d) % bands).wait_recv()
    for d in range(1, bands):
        first(d).wait_send()
        second(d, l).wait_send()


def image_kernel(sizes, part_ref, lat_ref, lon_ref, residual_ref, direction_ref, out_ref, coef_ref, own, there, far_out, near_out,
                 relay_out, far_in, near_in, relay_in, mine, band, halo, shard, everyone, res, dire, sums, line_got, line_sum,
                 send, recv, hsend, hrecv, psend, precv, rsend, rrecv, lsend, lrecv, load, local, fields, leave):
    o, l = lax.axis_index("obs"), lax.axis_index("lat")
    bands, weeks, count, bits, lat_decay, lon_decay = sizes
    z, c, at = obs_peers(o)
    partner, up, down = {"obs": at(0, 1 - c)}, {"obs": at(1, c)}, {"obs": at(-1, c)}
    k, side = 2 * CHIPS, CHIPS
    x, y = l // side, l % side
    lines = [[{"lat": x * side + (y + d) % side} for d in range(1, side)], [{"lat": (x + d) % side * side + y} for d in range(1, side)]]
    gets = [pltpu.make_async_copy(residual_ref, res, fields.at[0]), pltpu.make_async_copy(direction_ref, dire, fields.at[1])]
    greet([partner, up, down, {"lat": (l + 1) % bands}, {"lat": (l + bands - 1) % bands}, *lines[0], *lines[1]])
    order = (0, 2, 1, 3)

    def rows_for(core, w):
        return part_ref.at[:, core, w]

    swaps = [remote(rows_for(1 - c, w), there.at[w], (psend, precv), w, partner) for w in range(weeks)]
    loads = [pltpu.make_async_copy(rows_for(c, w), own.at[w], load.at[w]) for w in range(weeks)]
    for w in order:
        swaps[w].start()
        loads[w].start()
    for one in gets:
        one.start()
    sums[...] = jnp.zeros_like(sums)
    lon_width = down_rows(lon_ref, l * BAND)
    weights = lat_rows(lat_ref, lat_decay, l, bands, True)
    ring = (rsend, rrecv)

    def way(w):
        return (1, up, down) if w < 2 else (-1, down, up)

    far = [remote(far_out.at[w], far_in.at[w], ring, (0, w), way(w)[1]) for w in range(weeks)]
    relayed = [remote(relay_out.at[w], relay_in.at[w], ring, (1, w), way(w)[1]) for w in range(weeks)]
    near = [remote(near_out.at[w], near_in.at[w], ring, (2, w), way(w)[2]) for w in range(weeks)]
    halos = [halo_copies(band, halo, w, l, bands, (hsend, hrecv)) for w in range(weeks)]

    def chip_sum(w, step):
        there_too = (z + step + CHIPS) % CHIPS
        return [x + y for x, y in zip(blocks_of(own.at[w, there_too], count), blocks_of(there.at[w, there_too], count))]

    def plus(x, y):
        return [a + d for a, d in zip(x, y)]

    for w in order:
        swaps[w].wait_recv()
        loads[w].wait()
        encode(far_out.at[w], chip_sum(w, 2))
        far[w].start()
        encode(near_out.at[w], chip_sum(w, -way(w)[0]))
        near[w].start()
    gets[0].wait()
    for w in (0, 1):
        gram_first(k, count, w, res, sums)
    for w in order:
        far[w].wait_recv()
        encode(relay_out.at[w], plus(chip_sum(w, way(w)[0]), decode(far_in.at[w], count)))
        relayed[w].start()
    for w in order:
        if w == order[0]:
            for early in (2, 3):
                gram_first(k, count, early, res, sums)
            gets[1].wait()
        near[w].wait_recv()
        relayed[w].wait_recv()
        total = plus(plus(chip_sum(w, 0), decode(near_in.at[w], count)), decode(relay_in.at[w], count))
        encode(band.at[w], total)
        for one in halos[w]:
            one.start()
        put_blocks(mine.at[w], total)

    def produce(w):
        for one in halos[w]:
            one.wait_recv()
        stacks = stacks_of(decode(halo.at[0, w], count), blocks_of(mine.at[w], count), decode(halo.at[1, w], count))
        encode(shard.at[w], along_lon(mix_rows(weights, stacks), lon_width, lon_decay, bits))

    leaving = [pltpu.make_async_copy(everyone.at[:, w], out_ref.at[:, w], leave.at[w]) for w in range(weeks)]

    def consume(w):
        leaving[w].start()
        gram_week(k, count, w, res, dire, everyone, sums)

    run_gather(Gather(shard, everyone, o, (send, recv), local), order, produce, consume)
    total = gram_total(k, sums)
    for axis, here in ((0, y), (1, x)):
        line_sum[axis] = total
        copies = [remote(line_sum.at[axis], line_got.at[axis, here], (lsend, lrecv), (axis, d), to) for d, to in enumerate(lines[axis])]
        for one in copies:
            one.start()
        line_got[axis, here] = total
        for d in range(side - 1):
            back = (here + side - 1 - d) % side
            remote(line_sum.at[axis], line_got.at[axis, back], (lsend, lrecv), (axis, d), lines[axis][d]).wait_recv()
        total = line_got[axis, 0] + line_got[axis, 1] + line_got[axis, 2] + line_got[axis, 3]
        for one in copies:
            one.wait_send()
    coef_ref[...] = coefficients(total)
    for w in range(weeks):
        leaving[w].wait()
        for one in (swaps[w], far[w], relayed[w], near[w], *halos[w]):
            one.wait_send()


def change_block(change_ref, i, w, b, first, rows):
    at = b * BAND + first
    at = at if isinstance(at, int) else pl.multiple_of(at, 16)
    power = change_ref[i, w, WEEK:CODED, :].astype(jnp.int32).astype(F32)
    pick = jnp.sum(jnp.where(iota((16, EDGE), 0) == b, power, 0.0), axis=0, keepdims=True)
    return change_ref[i, w, pl.ds(at, rows), :].astype(jnp.int32).astype(F32) * (jnp.exp2(pick) * (1.0 / TOP))


def add_gram(sums, t, i, j, x, y):
    sums[t, i, j] = sums[t, i, j] + jnp.sum((x * y).reshape(BAND // 8, 8, EDGE), axis=0)


def lanes_of(b):
    return pl.ds(pl.multiple_of(b * EDGE, EDGE), EDGE)


def gram_first(k, count, w, res_ref, sums):
    def one(b, carry):
        res = [res_ref[i, w, :, lanes_of(b)] for i in range(k)]
        for i in range(k):
            for j in range(i, k):
                add_gram(sums, 0, i, j, res[i], res[j])
        return carry

    lax.fori_loop(0, count, one, 0)


def gram_week(k, count, w, res_ref, dire_ref, change_ref, sums):
    def one(b, carry):
        res = [res_ref[i, w, :, lanes_of(b)] for i in range(k)]
        dire = [dire_ref[i, w, :, lanes_of(b)] for i in range(k)]
        img = [dire[i] + change_block(change_ref, i, w, b, 0, BAND) for i in range(k)]
        for i in range(k):
            for j in range(k):
                if i <= j:
                    add_gram(sums, 3, i, j, img[i], img[j])
                add_gram(sums, 1, i, j, dire[i], img[j])
                add_gram(sums, 2, i, j, img[i], res[j])
        return carry

    lax.fori_loop(0, count, one, 0)


def gram_total(k, sums):
    lane = iota((k, EDGE), 1)
    result = jnp.zeros((k, EDGE), F32)
    for t in range(4):
        for i in range(k):
            line = jnp.sum(jnp.sum(sums[t, i], axis=1), axis=1, keepdims=True)
            result = jnp.where(lane == t * k + i, jnp.broadcast_to(line, (k, EDGE)), result)
    return result


def flip(x):
    square = jnp.concatenate([x, jnp.zeros((EDGE - 8, EDGE), F32)], axis=0)
    return jnp.transpose(square)[:8, :]


def product(x, y):
    return sum(jnp.broadcast_to(x[:, i:i + 1], (8, EDGE)) * jnp.broadcast_to(y[i:i + 1, :], (8, EDGE)) for i in range(8))


def solve(a, b):
    row = iota((8, EDGE), 0)
    for p in range(8):
        line = jnp.broadcast_to(a[p:p + 1, :], (8, EDGE))
        line_b = jnp.broadcast_to(b[p:p + 1, :], (8, EDGE))
        column = jnp.broadcast_to(a[:, p:p + 1], (8, EDGE))
        inverse = 1.0 / jnp.broadcast_to(a[p:p + 1, p:p + 1], (8, EDGE))
        ratio = column * inverse
        here = row == p
        a = jnp.where(here, line * inverse, a - ratio * line)
        b = jnp.where(here, line_b * inverse, b - ratio * line_b)
    return b


def coefficients(total):
    lane, row = iota((8, EDGE), 1), iota((8, EDGE), 0)
    parts = []
    for t in range(4):
        moved = total if t == 0 else pltpu.roll(total, EDGE - 8 * t, 1)
        parts.append(jnp.where(lane < 8, moved, 0.0))

    def full(x):
        low = jnp.where(lane <= row, x, 0.0)
        return low + flip(jnp.where(lane < row, x, 0.0))

    gram_old, image_image = full(parts[0]), full(parts[3])
    curvature = 0.5 * (parts[1] + flip(parts[1]))
    residual_image = parts[2]
    step = solve(curvature, gram_old)
    inverse = solve(gram_old, jnp.where(lane == row, 1.0, 0.0))
    cross = product(residual_image, step)
    gram_new = gram_old - cross - flip(cross) + product(flip(step), product(image_image, step))
    turn = product(inverse, gram_new)
    return jnp.where(lane < 8, step, 0.0) + pltpu.roll(jnp.where(lane < 8, turn, 0.0), 8, 1)


def update_kernel(k, coef_ref, solution_ref, residual_ref, direction_ref, change_ref, sol_out, res_out, dir_out):
    rows_each = 32

    def one(b, carry):
        lanes = pl.ds(pl.multiple_of(b * EDGE, EDGE), EDGE)
        for r in range(BAND // rows_each):
            rows = slice(r * rows_each, (r + 1) * rows_each)
            dire = [direction_ref[i, 0, rows, lanes] for i in range(k)]
            more = [change_block(change_ref, i, 0, b, r * rows_each, rows_each) for i in range(k)]
            for a in range(k):
                forth = sum(coef_ref[i, a] * dire[i] for i in range(k))
                back = sum(coef_ref[i, a] * more[i] for i in range(k))
                turn = sum(coef_ref[i, k + a] * dire[i] for i in range(k))
                left = residual_ref[a, 0, rows, lanes] - (forth + back)
                sol_out[a, 0, rows, lanes] = solution_ref[a, 0, rows, lanes] + forth
                res_out[a, 0, rows, lanes] = left
                dir_out[a, 0, rows, lanes] = left + turn
        return carry

    lax.fori_loop(0, 5, one, 0)


def params(collective=None, limit=None):
    extra = {} if collective is None else {"collective_id": collective, "has_side_effects": True}
    return pltpu.CompilerParams(vmem_limit_bytes=limit or (48 << 20), **extra)


def shards(bands, footprints, block_rows, block_cols, block_scale, lat_width, lon_width, obs_weight, solution, residual, direction):
    k, weeks, band_rows, nlon = direction.shape
    blocks = footprints.shape[2]
    count = nlon // EDGE
    assert (k, weeks, band_rows, count, bands) == (8, 4, BAND, 5, CHIPS * CHIPS)
    row_blocks = obs_weight.shape[0] // EDGE
    sizes = (bands, weeks, count, (nlon // 8 + 1).bit_length(), band_rows / 2.0, nlon / 32.0)
    all_rows = k * weeks * WEEK
    plain, coded = (weeks, WEEK, EDGE), (weeks, CODED, EDGE)
    ints = jnp.int16

    cells = pl.pallas_call(
        functools.partial(spread_kernel, sizes),
        out_shape=jax.ShapeDtypeStruct((k, *plain), BF16),
        in_specs=[ANY_SPEC, SMEM_SPEC, SMEM_SPEC],
        out_specs=ANY_SPEC,
        scratch_shapes=[
            VMEM((weeks, band_rows, nlon), F32), VMEM(plain, F32), VMEM(coded, ints), VMEM((2, *coded), ints), VMEM(plain, BF16),
            DMA((7, weeks)), DMA((7, weeks)), DMA((2, weeks)), DMA((2, weeks)), DMA((weeks,)), DMA((weeks,)),
        ],
        compiler_params=params(1, 64_450_000),
        name="spread",
    )(direction, lat_width, lon_width)

    blocks_held = [VMEM((blocks, EDGE, EDGE), BF16), DMA((blocks // CHUNK,))]
    smem = [SMEM_SPEC] * 3
    forward = pl.pallas_call(
        forward_kernel,
        out_shape=jax.ShapeDtypeStruct((row_blocks, k, EDGE), F32),
        in_specs=smem + [VMEM_SPEC, ANY_SPEC],
        out_specs=VMEM_SPEC,
        scratch_shapes=[VMEM((k * STEP, EDGE), F32), *blocks_held],
        compiler_params=params(),
        name="forward",
    )(block_rows, block_cols, block_scale, cells.reshape(all_rows, EDGE), footprints)

    share = row_blocks // bands
    values = pl.pallas_call(
        functools.partial(sum_bands_kernel, bands),
        out_shape=jax.ShapeDtypeStruct((row_blocks, k, EDGE), BF16),
        in_specs=[VMEM_SPEC, VMEM_SPEC],
        out_specs=VMEM_SPEC,
        scratch_shapes=[
            VMEM((bands, share, k, EDGE), F32), VMEM((share, k, EDGE), BF16),
            DMA((bands,)), DMA((bands,)), DMA((bands,)), DMA((bands,)),
        ],
        compiler_params=params(2),
        name="sum_bands",
    )(forward, obs_weight.reshape(row_blocks, 1, EDGE))

    part = pl.pallas_call(
        adjoint_kernel,
        out_shape=jax.ShapeDtypeStruct((all_rows, EDGE), F32),
        in_specs=smem + [VMEM_SPEC, ANY_SPEC],
        out_specs=VMEM_SPEC,
        scratch_shapes=[VMEM((k * STEP, EDGE), F32), *blocks_held],
        compiler_params=params(),
        name="adjoint",
    )(block_rows, block_cols, block_scale, values, footprints)

    side = CHIPS
    change, coef = pl.pallas_call(
        functools.partial(image_kernel, sizes),
        out_shape=[jax.ShapeDtypeStruct((k, *coded), ints), jax.ShapeDtypeStruct((k, EDGE), F32)],
        in_specs=[ANY_SPEC, SMEM_SPEC, SMEM_SPEC, ANY_SPEC, ANY_SPEC],
        out_specs=[ANY_SPEC, VMEM_SPEC],
        scratch_shapes=[
            VMEM((weeks, CHIPS, WEEK, EDGE), F32), VMEM((weeks, CHIPS, WEEK, EDGE), F32),
            *[VMEM(coded, ints)] * 6, VMEM(plain, F32), VMEM(coded, ints), VMEM((2, *coded), ints), VMEM(coded, ints),
            VMEM((k, *coded), ints), VMEM(direction.shape, F32), VMEM(direction.shape, F32), VMEM((4, k, k, 8, EDGE), F32),
            VMEM((2, side, k, EDGE), F32), VMEM((2, k, EDGE), F32),
            DMA((7, weeks)), DMA((7, weeks)), DMA((2, weeks)), DMA((2, weeks)), DMA((weeks,)), DMA((weeks,)),
            DMA((3, weeks)), DMA((3, weeks)), DMA((2, side - 1)), DMA((2, side - 1)), DMA((weeks,)), DMA((weeks,)),
            DMA((2,)), DMA((weeks,)),
        ],
        compiler_params=params(3),
        name="image",
    )(part.reshape(CHIPS, 2, *plain), lat_width, lon_width, residual, direction)

    native = pl.BlockSpec((k, 1, band_rows, nlon), lambda w: (0, w, 0, 0))
    packed = pl.BlockSpec((k, 1, CODED, EDGE), lambda w: (0, w, 0, 0))
    return pl.pallas_call(
        functools.partial(update_kernel, k),
        grid=(weeks,),
        out_shape=[jax.ShapeDtypeStruct(direction.shape, F32)] * 3,
        in_specs=[SMEM_SPEC, native, native, native, packed],
        out_specs=[native] * 3,
        compiler_params=params(),
        name="update",
    )(coef, solution, residual, direction, change)


def solution(mesh):
    assert mesh.shape["obs"] == 2 * CHIPS
    three = (P(None, None, "lat", None),) * 3
    blocks = P("obs", "lat", None)
    return jax.shard_map(
        functools.partial(shards, mesh.shape["lat"]),
        mesh=mesh,
        in_specs=(P("obs", "lat", None, None, None), blocks, blocks, blocks, P(), P(), P("obs"), *three),
        out_specs=three,
        check_vma=False,
    )
```
